256 devices in a mesh: segment: 8 (over z), ctx: 16 (over x, y), dp: 2 (over core).
Axes of the slice: x: 4, y: 4, z: 8, core: 2. Of those that a mesh axis runs over, the one named last changes fastest.
Arguments:
- frames_in: bfloat16 [2, 8, 2048, 1536], P('dp', None, 'ctx'), may hold values from -6 to 6
- lengths: int32 [2, 8], P('dp'), may hold values from 512 to 2048, as said below
- depth_kernel: float32 [8, 32, 1536], P('segment'), may hold values from -1 to 1
- batch_gain: float32 [8, 1536], P('segment'), may hold values from 0.25 to 1.75
- batch_bias: float32 [8, 1536], P('segment'), may hold values from -3 to 3
- out_weight: bfloat16 [8, 1536, 1536], P('segment', 'ctx'), may hold values from -0.15625 to 0.15625
Outputs:
- encoded: bfloat16 [2, 8, 2048, 1536], P('dp', 'segment', 'ctx')
The draws below stay inside these ranges and needn't reach their ends.
Inputs may be any that keep to these rules, and one draw needn't show every extreme that they name: `lengths`: valid frames of each utterance; in every draw some utterance has all 2048 frames.
All inputs are finite; a program needn't handle non-finite values.
Results may differ from the reference program's by a relative error of at most 0.017.
Values may be sent and summed in bfloat16 or wider, within the bound.
No kernel may reach another device: no remote copies, remote signals or barrier semaphores. Data moves between devices by JAX's collectives and lax.ppermute only.
A program may use at most 64 MiB of HBM per device.

```python
import jax
import jax.numpy as jnp
from jax import lax

D = 1536
K = 32
MICRO = 8
LAYERS = 8
FRAMES = 2048
REPL = 2


def draw_lengths(key, part):
    values = jax.random.randint(jax.random.fold_in(key, 11), (REPL * MICRO,), FRAMES // 4, FRAMES + 1)
    chosen = jax.random.randint(jax.random.fold_in(key, 12), (), 0, REPL * MICRO)
    places = jnp.arange(REPL * MICRO, dtype=jnp.int32)
    values = jnp.where(places == chosen, FRAMES, values)
    return values.reshape(REPL, MICRO).astype(jnp.int32)


def levels(stream_key, shape, split, least, largest):
    loudness = 1.0
    for axis_at, shards_of in split:
        draws = jax.random.uniform(jax.random.fold_in(jax.random.fold_in(stream_key, 6), axis_at), (shards_of,), jnp.float32, least / len(split), largest / len(split))
        loudness = loudness * jnp.repeat(jnp.exp(draws), shape[axis_at] // shards_of).reshape((-1,) + (1,) * (len(shape) - 1 - axis_at))
    return loudness


def scatter_about(rng, extent, scale, limit, shards=(), kind=jnp.bfloat16):
    drawn = jax.random.normal(rng, extent, jnp.float32) * scale
    if len(shards) > 0:
        drawn = levels(rng, extent, shards, -0.22, 0.18) * drawn
    return jnp.clip(drawn, min=-limit, max=limit).astype(kind)


def setup_inputs(seed: int = 0) -> dict:
    key_list = jax.random.split(jax.random.key(seed), 7)
    frames_in = scatter_about(key_list[0], (REPL, MICRO, FRAMES, D), 1.0, 6.0, ((0, 2), (2, 16)))
    lengths = draw_lengths(jax.random.fold_in(key_list[6], 71), 0)
    depth_kernel = scatter_about(key_list[2], (LAYERS, K, D), K ** -0.5, 1.0, ((0, 8),), jnp.float32)
    batch_gain = jnp.clip(1.0 + 0.15 * jax.random.normal(key_list[3], (LAYERS, D), jnp.float32), 0.25, 1.75)
    batch_bias = scatter_about(key_list[4], (LAYERS, D), 0.5, 3.0, ((0, 8),), jnp.float32)
    out_weight = scatter_about(key_list[5], (LAYERS, D, D), D ** -0.5, 0.15625, ((0, 8), (1, 16)))
    return dict(frames_in=frames_in, lengths=lengths, depth_kernel=depth_kernel, batch_gain=batch_gain, batch_bias=batch_bias, out_weight=out_weight)


EPSILON = 1e-05

def reference(frames_in, lengths, depth_kernel, batch_gain, batch_bias, out_weight):
    rim_width = K // 2
    frame_index = jnp.arange(FRAMES, dtype=jnp.int32)

    def one_batch(operands):
        state, utter_lens = operands
        valid = (frame_index[None, :] < utter_lens[:, None]).astype(jnp.float32)[..., None]
        frames_all = jnp.sum(valid)
        for layer_index in range(LAYERS):
            widened = state.astype(jnp.float32)
            frame_mean = lax.optimization_barrier(jnp.mean(widened, axis=2, keepdims=True))
            centred = widened - frame_mean
            frame_var = lax.optimization_barrier(jnp.mean(centred * centred, axis=2, keepdims=True))
            normed = (centred * lax.rsqrt(frame_var + EPSILON) * valid).astype(jnp.bfloat16)
            padded = jnp.pad(normed, ((0, 0), (rim_width, rim_width), (0, 0)))
            mixed = jnp.zeros(widened.shape, jnp.float32)
            for offset in range(K):
                mixed = mixed + padded[:, offset:offset + FRAMES].astype(jnp.float32) * depth_kernel[layer_index, offset]
            chan_mean = lax.optimization_barrier(jnp.sum(mixed * valid, axis=(0, 1))) / frames_all
            spread = mixed - chan_mean
            chan_var = lax.optimization_barrier(jnp.sum(valid * spread * spread, axis=(0, 1))) / frames_all
            scaled = spread * lax.rsqrt(chan_var + EPSILON) * batch_gain[layer_index] + batch_bias[layer_index]
            activation = (scaled * jax.nn.sigmoid(scaled) * valid).astype(jnp.bfloat16)
            product = jnp.dot(activation.reshape(-1, D), out_weight[layer_index], preferred_element_type=jnp.float32)
            state = (widened + product.reshape(widened.shape)).astype(jnp.bfloat16)
        return state
    finals = lax.map(one_batch, (jnp.swapaxes(frames_in, 0, 1), jnp.swapaxes(lengths, 0, 1)))
    return jnp.swapaxes(finals, 0, 1)
```

```python
import jax
import jax.numpy as jnp
from jax import lax
from jax.sharding import PartitionSpec as P

EPSILON = 1e-05


def shards(frames_in, lengths, depth_kernel, batch_gain, batch_bias, out_weight):
    layer_total = lax.axis_size("segment")
    ctx_count = lax.axis_size("ctx")
    segment_index = lax.axis_index("segment")
    ctx_index = lax.axis_index("ctx")
    dp_index = lax.axis_index("dp")
    frames_dev = frames_in.shape[2]
    model_width = frames_in.shape[3]
    kernel_size = depth_kernel.shape[1]
    rim = kernel_size // 2
    half_rows = out_weight.shape[1] // 2
    mine = lax.dynamic_slice_in_dim(out_weight[0], dp_index * half_rows, half_rows, 0)
    weights = lax.all_gather(mine, ("segment", "ctx", "dp"), axis=0, tiled=True)
    weights = weights.reshape(layer_total, model_width, model_width)
    params = jnp.concatenate([depth_kernel[0], batch_gain, batch_bias], axis=0)
    params = lax.all_gather(params, "segment", axis=0)

    both = [(0, 1), (1, 0)]
    mine_len = lax.dynamic_slice_in_dim(lengths[0], segment_index, 1, 0)
    count = (mine_len + lax.ppermute(mine_len, "dp", both)).astype(jnp.float32)
    frame_index = ctx_index * frames_dev + jnp.arange(frames_dev, dtype=jnp.int32)
    valid = (frame_index < mine_len).astype(jnp.float32)[:, None]
    state = lax.dynamic_index_in_dim(frames_in[0], segment_index, 0, keepdims=False)

    forward = [(i, i + 1) for i in range(ctx_count - 1)]
    backward = [(b, a) for a, b in forward]
    for layer in range(layer_total):
        taps = params[layer, :kernel_size]
        gain = params[layer, kernel_size]
        bias = params[layer, kernel_size + 1]
        widened = state.astype(jnp.float32)
        frame_mean = jnp.mean(widened, axis=1, keepdims=True)
        centred = widened - frame_mean
        frame_var = jnp.mean(centred * centred, axis=1, keepdims=True)
        normed = (centred * lax.rsqrt(frame_var + EPSILON) * valid).astype(jnp.bfloat16)
        low = lax.ppermute(normed[frames_dev - rim :], "ctx", forward)
        high = lax.ppermute(normed[:rim], "ctx", backward)
        padded = jnp.concatenate([low, normed, high], axis=0)
        mixed = jnp.zeros(widened.shape, jnp.float32)
        for offset in range(kernel_size):
            mixed = mixed + padded[offset : offset + frames_dev].astype(jnp.float32) * taps[offset]
        masked = mixed * valid
        sums = jnp.stack([jnp.sum(masked, axis=0), jnp.sum(masked * mixed, axis=0)])
        sums = sums + lax.ppermute(sums, "dp", both)
        sums = lax.all_to_all(
            jnp.broadcast_to(sums[None], (ctx_count, *sums.shape)), "ctx", 0, 0, tiled=True
        ).sum(axis=0)
        chan_mean = sums[0] / count
        chan_var = sums[1] / count - chan_mean * chan_mean
        scaled = (mixed - chan_mean) * (lax.rsqrt(chan_var + EPSILON) * gain) + bias
        activation = (scaled * jax.nn.sigmoid(scaled) * valid).astype(jnp.bfloat16)
        product = jnp.dot(activation, weights[layer], preferred_element_type=jnp.float32)
        state = (widened + product).astype(jnp.bfloat16)
    return state[None, None]


def solution(mesh):
    placed = (
        P("dp", None, "ctx", None),
        P("dp", None),
        P("segment", None, None),
        P("segment", None),
        P("segment", None),
        P("segment", "ctx", None),
    )
    return jax.shard_map(
        shards,
        mesh=mesh,
        in_specs=placed,
        out_specs=P("dp", "segment", "ctx", None),
        check_vma=False,
    )
```

```python
import functools
import jax
import jax.numpy as jnp
from jax import lax
from jax.experimental import pallas as pl
from jax.experimental.pallas import tpu as pltpu
from jax.sharding import PartitionSpec as P

EPSILON = 1e-05
LANES = 128


def module_kernel(do_mm, do_conv, rim, taps_n, chunks, w_row, *refs):
    refs = list(refs)
    scal = refs.pop(0)
    if do_mm:
        mixed, low, high = refs.pop(0), refs.pop(0), refs.pop(0)
        sums = refs.pop(0)
        gain_bias, w_hbm = refs.pop(0), refs.pop(0)
    state = refs.pop(0)
    if do_conv:
        taps = refs.pop(0)
    state_out = refs.pop(0)
    if do_conv:
        mixed_out, sums_out, edge_low, edge_high = [refs.pop(0) for _ in range(4)]
    if do_mm:
        act_s, w_s, sems = refs.pop(0), refs.pop(0), refs.pop(0)
    if do_conv:
        norm_s, mask_s = refs.pop(0), refs.pop(0)

    ext, width = state.shape
    own = ext - 2 * rim
    length = scal[0]
    first = scal[1]
    lane_groups = width // LANES

    def row_valid(row, rows, lanes):
        at = lax.broadcasted_iota(jnp.int32, (rows, lanes), 0) + (first + row)
        return jnp.where((at >= 0) & (at < length), 1.0, 0.0).astype(jnp.float32)

    if do_mm:
        wide = width // chunks
        copies = []
        for n in range(chunks):
            lanes = pl.ds(n * wide, wide)
            copies.append(
                pltpu.make_async_copy(
                    w_hbm.at[pl.ds(w_row, width), lanes], w_s.at[:, lanes], sems.at[n]
                )
            )
            copies[-1].start()
        total = sums[0]
        for s in range(1, sums.shape[0]):
            total = total + sums[s]
        count = scal[2].astype(jnp.float32)
        mean = total[0:1] / count
        var = total[1:2] / count - mean * mean
        scale = lax.rsqrt(var + EPSILON) * gain_bias[0:1]
        shift = gain_bias[1:2] - mean * scale
        scale, shift = 0.5 * scale, 0.5 * shift

        for g in range(lane_groups):
            lanes = slice(g * LANES, (g + 1) * LANES)
            sc, sh = scale[:, lanes], shift[:, lanes]
            for src, row, rows in ((low, 0, rim), (mixed, rim, own), (high, rim + own, rim)):
                half = src[:, lanes].astype(jnp.float32) * sc + sh
                act = (half + half * jnp.tanh(half)) * row_valid(row, rows, LANES)
                act_s[row : row + rows, lanes] = act.astype(jnp.bfloat16)
        top = 0 if do_conv else rim
        rows = ext if do_conv else own
        for n in range(chunks):
            lanes = slice(n * wide, (n + 1) * wide)
            copies[n].wait()
            product = jnp.dot(
                act_s[top : top + rows, :], w_s[:, lanes], preferred_element_type=jnp.float32
            )
            old = state[top : top + rows, lanes].astype(jnp.float32)
            state_out[:, lanes] = (old + product).astype(jnp.bfloat16)
    elif do_conv:
        state_out[...] = state[...]

    if do_conv:
        block = 16

        def norm_rows(i, carry):
            row = pl.multiple_of(i * block, block)
            x = state_out[pl.ds(row, block), :].astype(jnp.float32)
            mean = jnp.mean(x, axis=1, keepdims=True)
            x = x - mean
            var = jnp.mean(x * x, axis=1, keepdims=True)
            y = x * (lax.rsqrt(var + EPSILON) * row_valid(row, block, 1))
            norm_s[pl.ds(row, block), :] = y.astype(jnp.bfloat16).astype(jnp.float32)
            return carry

        lax.fori_loop(0, ext // block, norm_rows, 0)
        mask_s[...] = row_valid(rim, own, LANES)

        def conv_lanes(g, carry):
            lanes = pl.ds(pl.multiple_of(g * LANES, LANES), LANES)
            tap = [jnp.broadcast_to(taps[k : k + 1, lanes], (8, LANES)) for k in range(taps_n)]
            tiles = own // 8
            acc = [None] * tiles
            for at in range(8 * (tiles - 1) + taps_n):
                v = norm_s[pl.ds(at, 8), lanes]
                for i in range(tiles):
                    k = at - 8 * i
                    if 0 <= k < taps_n:
                        term = tap[k] * v
                        acc[i] = term if acc[i] is None else acc[i] + term
            one = two = None
            for i in range(tiles):
                mixed_out[8 * i : 8 * i + 8, lanes] = acc[i]
                m = acc[i] * mask_s[8 * i : 8 * i + 8, :]
                q = m * acc[i]
                one = m if one is None else one + m
                two = q if two is None else two + q
            sums_out[0:1, lanes] = jnp.sum(one, axis=0, keepdims=True)
            sums_out[1:2, lanes] = jnp.sum(two, axis=0, keepdims=True)
            edge_low[:, lanes] = mixed_out[0:rim, lanes].astype(jnp.bfloat16)
            edge_high[:, lanes] = mixed_out[own - rim : own, lanes].astype(jnp.bfloat16)
            return carry

        lax.fori_loop(0, lane_groups, conv_lanes, 0)


def run_module(scal, state, prev=None, taps=None, w_row=0):
    ext, width = state.shape
    rim = 16
    own = ext - 2 * rim
    chunks = 6
    do_mm, do_conv = prev is not None, taps is not None
    vmem = pl.BlockSpec(memory_space=pltpu.VMEM)
    args, specs = [scal], [pl.BlockSpec(memory_space=pltpu.SMEM)]
    scratch = []
    if do_mm:
        mixed, low, high, sums, gain_bias, w = prev
        args += [mixed, low, high, sums, gain_bias]
        specs += [vmem] * 5
        args.append(w)
        specs.append(pl.BlockSpec(memory_space=pl.ANY))
        scratch += [
            pltpu.VMEM((ext, width), jnp.bfloat16),
            pltpu.VMEM((width, width), jnp.bfloat16),
            pltpu.SemaphoreType.DMA((chunks,)),
        ]
    args.append(state)
    specs.append(vmem)
    taps_n = 0
    if do_conv:
        taps_n = taps.shape[0]
        args.append(taps)
        specs.append(vmem)
        scratch += [pltpu.VMEM((ext, width), jnp.float32), pltpu.VMEM((own, LANES), jnp.float32)]
        shapes = [
            jax.ShapeDtypeStruct((ext, width), jnp.bfloat16),
            jax.ShapeDtypeStruct((own, width), jnp.float32),
            jax.ShapeDtypeStruct((2, width), jnp.float32),
            jax.ShapeDtypeStruct((rim, width), jnp.bfloat16),
            jax.ShapeDtypeStruct((rim, width), jnp.bfloat16),
        ]
    else:
        shapes = [jax.ShapeDtypeStruct((own, width), jnp.bfloat16)]
    return pl.pallas_call(
        functools.partial(module_kernel, do_mm, do_conv, rim, taps_n, chunks, w_row),
        out_shape=shapes,
        in_specs=specs,
        out_specs=[vmem] * len(shapes),
        scratch_shapes=scratch,
        compiler_params=pltpu.CompilerParams(vmem_limit_bytes=24 << 20),
        name="module_step",
    )(*args)


def shards(frames_in, lengths, depth_kernel, batch_gain, batch_bias, out_weight):
    layer_total = lax.axis_size("segment")
    ctx_count = lax.axis_size("ctx")
    segment_index = lax.axis_index("segment")
    ctx_index = lax.axis_index("ctx")
    dp_index = lax.axis_index("dp")
    frames_dev = frames_in.shape[2]
    width = frames_in.shape[3]
    kernel_size = depth_kernel.shape[1]
    rim = kernel_size // 2
    both = [(0, 1), (1, 0)]
    forward = [(i, i + 1) for i in range(ctx_count - 1)]
    backward = [(b, a) for a, b in forward]

    half_rows = out_weight.shape[1] // 2
    mine = lax.dynamic_slice_in_dim(out_weight[0], dp_index * half_rows, half_rows, 0)
    weights = lax.all_gather(mine, ("segment", "ctx", "dp"), axis=0, tiled=True)
    params = jnp.concatenate([depth_kernel[0], batch_gain, batch_bias], axis=0)
    params = lax.all_gather(params, "segment", axis=0)

    mine_len = lax.dynamic_slice_in_dim(lengths[0], segment_index, 1, 0)
    count = mine_len + lax.ppermute(mine_len, "dp", both)
    first = (ctx_index * frames_dev - rim).astype(jnp.int32)
    scal = jnp.concatenate([mine_len, first[None], count])

    def around(to_low, to_high):
        low = lax.ppermute(to_high, "ctx", forward)
        high = lax.ppermute(to_low, "ctx", backward)
        return low, high

    own = lax.dynamic_index_in_dim(frames_in[0], segment_index, 0, keepdims=False)
    low, high = around(own[:rim], own[frames_dev - rim :])
    state = jnp.concatenate([low, own, high], axis=0)

    prev = None
    for layer in range(layer_total):
        taps = params[layer, :kernel_size]
        state, mixed, sums, edge_low, edge_high = run_module(
            scal, state, prev, taps, (layer - 1) * width
        )
        low, high = around(edge_low, edge_high)
        sums = sums + lax.ppermute(sums, "dp", both)
        sums = lax.all_to_all(
            jnp.broadcast_to(sums[None], (ctx_count, *sums.shape)), "ctx", 0, 0, tiled=True
        )
        gain_bias = params[layer, kernel_size:]
        prev = (mixed, low, high, sums, gain_bias, weights)
    (state,) = run_module(scal, state, prev, None, (layer_total - 1) * width)
    return state[None, None]


def solution(mesh):
    placed = (
        P("dp", None, "ctx", None),
        P("dp", None),
        P("segment", None, None),
        P("segment", None),
        P("segment", None),
        P("segment", "ctx", None),
    )
    return jax.shard_map(
        shards,
        mesh=mesh,
        in_specs=placed,
        out_specs=P("dp", "segment", "ctx", None),
        check_vma=False,
    )
```

```python
import functools

import jax
import jax.numpy as jnp
from jax import lax
from jax.experimental import pallas as pl
from jax.experimental.pallas import tpu as pltpu
from jax.sharding import PartitionSpec as P

EPSILON = 1e-05
LANES = 128
SUBLANES = 8


def module_kernel(plan, *refs):
    do_mm, do_conv, layer, act_rows, own, first_at, chunks, group_at, taps_n, blocks = plan
    refs = list(refs)
    scal = refs.pop(0)
    if do_mm:
        mixed, sums, others, gain_bias = [refs.pop(0) for _ in range(4)]
        w_parts = [refs.pop(0) for _ in range(max(1, len(blocks)))]
    state = refs.pop(0)
    if do_conv:
        z_hbm = refs.pop(0)
    state_out = refs.pop(0)
    if do_conv:
        mixed_out, sums_out = refs.pop(0), refs.pop(0)
    if do_mm:
        act_s, w_s, sems = refs.pop(0), refs.pop(0), refs.pop(0)
    if do_conv:
        norm_s, mask_s, mix_s, taps, tap_sem = [refs.pop(0) for _ in range(5)]
        at = z_hbm.shape[1] - taps_n
        tap_copy = pltpu.make_async_copy(z_hbm.at[layer, pl.ds(at, taps_n)], taps, tap_sem.at[0])
        tap_copy.start()

    width = state.shape[1]
    length = scal[0]
    first = scal[1] + first_at
    lane_groups = width // LANES

    def row_valid(row, rows, lanes):
        at = lax.broadcasted_iota(jnp.int32, (rows, lanes), 0) + (first + row)
        return jnp.where((at >= 0) & (at < length), 1.0, 0.0).astype(jnp.float32)

    if do_mm:
        wide = width // chunks
        copies = []
        if blocks:
            for part, count in zip(w_parts, blocks):
                for i in range(count):
                    n = len(copies)
                    copies.append(
                        pltpu.make_async_copy(
                            part.at[i, group_at], w_s.at[scal[3 + n]], sems.at[n]
                        )
                    )
        else:
            for n in range(chunks):
                lanes = pl.ds(n * wide, wide)
                copies.append(
                    pltpu.make_async_copy(
                        w_parts[0].at[:, group_at, :, lanes], w_s.at[:, :, lanes], sems.at[n]
                    )
                )
        for copy in copies:
            copy.start()
        total = sums[0] + others[0]
        for s in range(1, sums.shape[0]):
            total = total + sums[s] + others[s]
        count = scal[2].astype(jnp.float32)
        mean = total[0:1] / count
        var = total[1:2] / count - mean * mean
        scale = lax.rsqrt(var + EPSILON) * gain_bias[layer - 1, 0:1]
        shift = gain_bias[layer - 1, 1:2] - mean * scale
        scale, shift = 0.5 * scale, 0.5 * shift
        valid = row_valid(0, act_rows, LANES)
        for g in range(lane_groups):
            lanes = slice(g * LANES, (g + 1) * LANES)
            half = mixed[:, lanes].astype(jnp.float32) * scale[:, lanes] + shift[:, lanes]
            act = (half + half * jnp.tanh(half)) * valid
            act_s[:, lanes] = act.astype(jnp.bfloat16)
        top = (state.shape[0] - act_rows) // 2
        if blocks:
            for copy in copies:
                copy.wait()
        for n in range(chunks):
            lanes = slice(n * wide, (n + 1) * wide)
            if not blocks:
                copies[n].wait()
            rows = w_s[:, :, lanes].reshape(width, wide)
            product = jnp.dot(act_s[...], rows, preferred_element_type=jnp.float32)
            old = state[top : top + act_rows, lanes].astype(jnp.float32)
            state_out[:, lanes] = (old + product).astype(jnp.bfloat16)
        normed_from = state_out
    else:
        state_out[...] = state[...]
        normed_from = state

    if do_conv:
        block = 32

        def norm_rows(i, carry):
            row = pl.multiple_of(i * block, block)
            x = normed_from[pl.ds(row, block), :].astype(jnp.float32)
            mean = jnp.mean(x, axis=1, keepdims=True)
            x = x - mean
            var = jnp.mean(x * x, axis=1, keepdims=True)
            y = x * (lax.rsqrt(var + EPSILON) * row_valid(row, block, 1))
            y = y.astype(jnp.bfloat16).astype(jnp.float32)
            for g in range(lane_groups):
                norm_s[g, pl.ds(row, block), :] = y[:, g * LANES : (g + 1) * LANES]
            return carry

        lax.fori_loop(0, act_rows // block, norm_rows, 0)
        tap_copy.wait()
        out_rows = act_rows - taps_n
        edge = (out_rows - own) // 2
        mask_s[...] = row_valid(edge + taps_n // 2, own, LANES)
        tiles = out_rows // SUBLANES
        splits = 1 if tiles <= 24 else 2
        run = tiles // splits

        def conv_lanes(g, carry):
            lanes = pl.ds(pl.multiple_of(g * LANES, LANES), LANES)
            for b in range(splits):
                base = b * run * SUBLANES
                tap = [
                    jnp.broadcast_to(taps[k : k + 1, lanes].astype(jnp.float32), (SUBLANES, LANES))
                    for k in range(taps_n)
                ]
                acc = [None] * run
                for m in range(run + taps_n - 1):
                    v = norm_s[g, pl.ds(base + m, SUBLANES, stride=run), :]
                    for j in range(run):
                        if 0 <= m - j < taps_n:
                            term = tap[m - j] * v
                            acc[j] = term if acc[j] is None else acc[j] + term
                for j in range(run):
                    mix_s[pl.ds(base + j, SUBLANES, stride=run), :] = acc[j]
            mixed_out[:, lanes] = mix_s[...].astype(jnp.bfloat16)
            mine = mix_s[edge : edge + own, :]
            masked = mine * mask_s[...]
            one = jnp.sum(masked, axis=0, keepdims=True)
            two = jnp.sum(masked * mine, axis=0, keepdims=True)
            both = jnp.concatenate([one, two], axis=0)
            for c in range(sums_out.shape[0]):
                sums_out[c, :, lanes] = both
            return carry

        lax.fori_loop(0, lane_groups, conv_lanes, 0)


def run_module(scal, state, own, layer, rim, copies, prev=None, z=None):
    width = state.shape[1]
    chunks = 6
    taps_n = 2 * rim
    do_mm, do_conv = prev is not None, z is not None
    vmem = pl.BlockSpec(memory_space=pltpu.VMEM)
    hbm = pl.BlockSpec(memory_space=pl.ANY)
    args, specs = [scal], [pl.BlockSpec(memory_space=pltpu.SMEM)]
    scratch = []
    group_at, blocks = 0, ()
    act_rows = state.shape[0]
    if do_mm:
        mixed, sums, others, gain_bias, parts, group_at = prev
        act_rows = mixed.shape[0]
        args += [mixed, sums, others, gain_bias, *parts]
        specs += [vmem] * 4 + [hbm] * len(parts)
        rows = parts[0].shape[2]
        if len(parts) > 1:
            blocks = tuple(p.shape[0] for p in parts)
        scratch += [
            pltpu.VMEM((act_rows, width), jnp.bfloat16),
            pltpu.VMEM((width // rows, rows, width), jnp.bfloat16),
            pltpu.SemaphoreType.DMA((max(chunks, sum(blocks)),)),
        ]
    args.append(state)
    specs.append(vmem)
    shapes = [jax.ShapeDtypeStruct((act_rows, width), jnp.bfloat16)]
    if do_conv:
        args.append(z)
        specs.append(hbm)
        out_rows = act_rows - taps_n
        scratch += [
            pltpu.VMEM((width // LANES, act_rows, LANES), jnp.float32),
            pltpu.VMEM((own, LANES), jnp.float32),
            pltpu.VMEM((out_rows, LANES), jnp.float32),
            pltpu.VMEM((taps_n, width), z.dtype),
            pltpu.SemaphoreType.DMA((1,)),
        ]
        shapes += [
            jax.ShapeDtypeStruct((out_rows, width), jnp.bfloat16),
            jax.ShapeDtypeStruct((copies, 2, width), jnp.float32),
        ]
    plan = (
        do_mm, do_conv, layer, act_rows, own, layer * rim, chunks, group_at, taps_n, blocks
    )
    return pl.pallas_call(
        functools.partial(module_kernel, plan),
        out_shape=shapes,
        in_specs=specs,
        out_specs=[vmem] * len(shapes),
        scratch_shapes=scratch,
        compiler_params=pltpu.CompilerParams(vmem_limit_bytes=26 << 20),
        name="module_step",
    )(*args)


SIDE = 4
STEPS = (0, 1, 3, 2)


def line_shift(steps, turned):
    pairs = []
    for p in range(SIDE):
        for q in range(SIDE):
            for core in range(2):
                to = (p, (q + steps) % SIDE) if core != turned else ((p + steps) % SIDE, q)
                pairs.append(((p * SIDE + q) * 2 + core, (to[0] * SIDE + to[1]) * 2 + core))
    return pairs


def plane_gather(mine):
    names = ("ctx", "dp")

    def along(x, steps):
        return lax.ppermute(x, names, line_shift(steps, 0))

    def across(x, steps):
        return lax.ppermute(x, names, line_shift(steps, 1))

    line = jnp.stack([mine] + [along(mine, steps) for steps in STEPS[1:]])
    half = SIDE // 2
    ahead, behind = across(line, 1), across(line, SIDE - 1)
    far = [across(ahead[:half], 1), across(behind[half:], SIDE - 1)]
    parts = [line, ahead, behind, *far]
    return parts + [lax.ppermute(p, "dp", [(0, 1), (1, 0)]) for p in parts]


def plane_places(ctx_index, dp_index):
    x, y = ctx_index // SIDE, ctx_index % SIDE
    half = SIDE // 2
    places = []
    for core in (dp_index, 1 - dp_index):
        p, q = jnp.where(core == 0, x, y), jnp.where(core == 0, y, x)
        for across, moved in ((0, STEPS), (1, STEPS), (3, STEPS), (2, STEPS[:half]), (2, STEPS[half:])):
            for steps in moved:
                a, b = (p - steps) % SIDE, (q - across) % SIDE
                at = jnp.where(core == 0, a * SIDE + b, b * SIDE + a)
                places.append(at * 2 + core)
    return jnp.stack(places).astype(jnp.int32)


EARLY = ((0, 1), (1, 3))


def shards(frames_in, lengths, depth_kernel, batch_gain, batch_bias, out_weight):
    layer_total = lax.axis_size("segment")
    ctx_count = lax.axis_size("ctx")
    segment_index = lax.axis_index("segment")
    ctx_index = lax.axis_index("ctx")
    dp_index = lax.axis_index("dp")
    frames_dev = frames_in.shape[2]
    kernel_size = depth_kernel.shape[1]
    rim = kernel_size // 2
    both = [(0, 1), (1, 0)]
    forward = [(i, i + 1) for i in range(ctx_count - 1)]
    backward = [(b, a) for a, b in forward]

    half_rows = out_weight.shape[1] // 2
    mine = lax.dynamic_slice_in_dim(out_weight[0], dp_index * half_rows, half_rows, 0)
    z = jnp.concatenate([mine, depth_kernel[0].astype(jnp.bfloat16)], axis=0)
    z = lax.all_gather(z, "segment", axis=0)
    gain_bias = lax.all_gather(jnp.concatenate([batch_gain, batch_bias], axis=0), "segment", axis=0)

    mine_len = lax.dynamic_slice_in_dim(lengths[0], segment_index, 1, 0)
    count = mine_len + lax.ppermute(mine_len, "dp", both)
    halo = rim * layer_total
    first = (ctx_index * frames_dev - halo).astype(jnp.int32)
    scal = jnp.concatenate([mine_len, first[None], count, plane_places(ctx_index, dp_index)])

    own = lax.dynamic_index_in_dim(frames_in[0], segment_index, 0, keepdims=False)
    low = lax.ppermute(own[frames_dev - halo :], "ctx", forward)
    high = lax.ppermute(own[:halo], "ctx", backward)
    state = jnp.concatenate([low, own, high], axis=0)

    rows = z[:, :half_rows]
    weights = {}
    for lo, hi in EARLY:
        parts = plane_gather(rows[lo:hi])
        for layer in range(lo, hi):
            weights[layer] = (parts, layer - lo)
    late = EARLY[-1][1]
    parts = [lax.all_gather(rows[late:], ("ctx", "dp"), axis=0)]
    for layer in range(late, layer_total):
        weights[layer] = (parts, layer - late)

    prev = None
    for layer in range(layer_total):
        state, mixed, sums = run_module(
            scal, state, frames_dev, layer, rim, ctx_count, prev, z
        )
        sums = lax.all_to_all(sums, "ctx", 0, 0, tiled=True)
        others = lax.ppermute(sums, "dp", both)
        prev = (mixed, sums, others, gain_bias, *weights[layer])
    (state,) = run_module(scal, state, frames_dev, layer_total, rim, ctx_count, prev)
    return state[None, None]


def solution(mesh):
    placed = (
        P("dp", None, "ctx", None),
        P("dp", None),
        P("segment", None, None),
        P("segment", None),
        P("segment", None),
        P("segment", "ctx", None),
    )
    return jax.shard_map(
        shards,
        mesh=mesh,
        in_specs=placed,
        out_specs=P("dp", "segment", "ctx", None),
        check_vma=False,
    )
```

```python
import functools

import jax
import jax.numpy as jnp
from jax import lax
from jax.experimental import pallas as pl
from jax.experimental.pallas import tpu as pltpu
from jax.sharding import PartitionSpec as P

EPSILON = 1e-05
LANES = 128
SUBLANES = 8
EXTRA = 8


def module_kernel(plan, *refs):
    do_mm, do_conv, layer, act_rows, own, first_at, chunks, group_at, taps_n, blocks = plan
    refs = list(refs)
    scal = refs.pop(0)
    if do_mm:
        mixed, sums, others = [refs.pop(0) for _ in range(3)]
        w_parts = [refs.pop(0) for _ in range(max(1, len(blocks)))]
    state, z_hbm = refs.pop(0), refs.pop(0)
    state_out = refs.pop(0)
    if do_conv:
        mixed_out, sums_out = refs.pop(0), refs.pop(0)
    if do_mm:
        act_s, w_s, sems, gb, gb_sem = [refs.pop(0) for _ in range(5)]
        at = z_hbm.shape[1] - EXTRA
        gb_copy = pltpu.make_async_copy(z_hbm.at[layer - 1, pl.ds(at, EXTRA)], gb, gb_sem.at[0])
        gb_copy.start()
    if do_conv:
        norm_s, mask_s, mix_s, taps, tap_sem = [refs.pop(0) for _ in range(5)]
        at = z_hbm.shape[1] - EXTRA - taps_n
        tap_copy = pltpu.make_async_copy(z_hbm.at[layer, pl.ds(at, taps_n)], taps, tap_sem.at[0])
        tap_copy.start()

    width = state.shape[1]
    length = scal[0]
    first = scal[1] + first_at
    lane_groups = width // LANES

    def row_valid(row, rows, lanes):
        at = lax.broadcasted_iota(jnp.int32, (rows, lanes), 0) + (first + row)
        return jnp.where((at >= 0) & (at < length), 1.0, 0.0).astype(jnp.float32)

    if do_mm:
        wide = width // chunks
        copies = []
        if blocks:
            for part, count in zip(w_parts, blocks):
                for i in range(count):
                    n = len(copies)
                    copies.append(
                        pltpu.make_async_copy(
                            part.at[i, group_at], w_s.at[scal[3 + n]], sems.at[n]
                        )
                    )
        else:
            for n in range(chunks):
                lanes = pl.ds(n * wide, wide)
                copies.append(
                    pltpu.make_async_copy(
                        w_parts[0].at[:, group_at, :, lanes], w_s.at[:, :, lanes], sems.at[n]
                    )
                )
        for copy in copies:
            copy.start()
        total = sums[0] + others[0]
        for s in range(1, sums.shape[0]):
            total = total + sums[s] + others[s]
        count = scal[2].astype(jnp.float32)
        mean = total[0:1] / count
        var = total[1:2] / count - mean * mean
        gb_copy.wait()
        halves = gb[...].astype(jnp.float32)
        scale = lax.rsqrt(var + EPSILON) * (halves[0:1] + halves[1:2])
        shift = (halves[2:3] + halves[3:4]) - mean * scale
        scale, shift = 0.5 * scale, 0.5 * shift
        valid = row_valid(0, act_rows, LANES)
        for g in range(lane_groups):
            lanes = slice(g * LANES, (g + 1) * LANES)
            half = mixed[:, lanes].astype(jnp.float32) * scale[:, lanes] + shift[:, lanes]
            act = (half + half * jnp.tanh(half)) * valid
            act_s[:, lanes] = act.astype(jnp.bfloat16)
        top = (state.shape[0] - act_rows) // 2
        if blocks:
            for copy in copies:
                copy.wait()
        for n in range(chunks):
            lanes = slice(n * wide, (n + 1) * wide)
            if not blocks:
                copies[n].wait()
            rows = w_s[:, :, lanes].reshape(width, wide)
            product = jnp.dot(act_s[...], rows, preferred_element_type=jnp.float32)
            old = state[top : top + act_rows, lanes].astype(jnp.float32)
            state_out[:, lanes] = (old + product).astype(jnp.bfloat16)
        normed_from = state_out
    else:
        state_out[...] = state[...]
        normed_from = state

    if do_conv:
        block = 32

        def norm_rows(i, carry):
            row = pl.multiple_of(i * block, block)
            x = normed_from[pl.ds(row, block), :].astype(jnp.float32)
            mean = jnp.mean(x, axis=1, keepdims=True)
            x = x - mean
            var = jnp.mean(x * x, axis=1, keepdims=True)
            y = x * (lax.rsqrt(var + EPSILON) * row_valid(row, block, 1))
            y = y.astype(jnp.bfloat16).astype(jnp.float32)
            for g in range(lane_groups):
                norm_s[g, pl.ds(row, block), :] = y[:, g * LANES : (g + 1) * LANES]
            return carry

        lax.fori_loop(0, act_rows // block, norm_rows, 0)
        tap_copy.wait()
        out_rows = act_rows - taps_n
        edge = (out_rows - own) // 2
        mask_s[...] = row_valid(edge + taps_n // 2, own, LANES)
        tiles = out_rows // SUBLANES
        splits = 1 if tiles <= 24 else 2
        run = tiles // splits

        def conv_lanes(g, carry):
            lanes = pl.ds(pl.multiple_of(g * LANES, LANES), LANES)
            for b in range(splits):
                base = b * run * SUBLANES
                tap = [
                    jnp.broadcast_to(taps[k : k + 1, lanes].astype(jnp.float32), (SUBLANES, LANES))
                    for k in range(taps_n)
                ]
                acc = [None] * run
                for m in range(run + taps_n - 1):
                    v = norm_s[g, pl.ds(base + m, SUBLANES, stride=run), :]
                    for j in range(run):
                        if 0 <= m - j < taps_n:
                            term = tap[m - j] * v
                            acc[j] = term if acc[j] is None else acc[j] + term
                for j in range(run):
                    mix_s[pl.ds(base + j, SUBLANES, stride=run), :] = acc[j]
            mixed_out[:, lanes] = mix_s[...].astype(jnp.bfloat16)
            mine = mix_s[edge : edge + own, :]
            masked = mine * mask_s[...]
            one = jnp.sum(masked, axis=0, keepdims=True)
            two = jnp.sum(masked * mine, axis=0, keepdims=True)
            both = jnp.concatenate([one, two], axis=0)
            for c in range(sums_out.shape[0]):
                sums_out[c, :, lanes] = both
            return carry

        lax.fori_loop(0, lane_groups, conv_lanes, 0)


def run_module(scal, state, z, own, layer, rim, copies, prev, do_conv):
    width = state.shape[1]
    chunks = 6
    taps_n = 2 * rim
    do_mm = prev is not None
    vmem = pl.BlockSpec(memory_space=pltpu.VMEM)
    hbm = pl.BlockSpec(memory_space=pltpu.HBM)
    args, specs = [scal], [pl.BlockSpec(memory_space=pltpu.SMEM)]
    scratch = []
    group_at, blocks = 0, ()
    act_rows = state.shape[0]
    if do_mm:
        mixed, sums, others, parts, group_at = prev
        act_rows = mixed.shape[0]
        args += [mixed, sums, others, *parts]
        specs += [vmem] * 3 + [hbm] * len(parts)
        rows = parts[0].shape[2]
        if len(parts) > 1:
            blocks = tuple(p.shape[0] for p in parts)
        scratch += [
            pltpu.VMEM((act_rows, width), jnp.bfloat16),
            pltpu.VMEM((width // rows, rows, width), jnp.bfloat16),
            pltpu.SemaphoreType.DMA((max(chunks, sum(blocks)),)),
            pltpu.VMEM((EXTRA, width), z.dtype),
            pltpu.SemaphoreType.DMA((1,)),
        ]
    args += [state, z]
    specs += [vmem, hbm]
    shapes = [jax.ShapeDtypeStruct((act_rows, width), jnp.bfloat16)]
    if do_conv:
        out_rows = act_rows - taps_n
        scratch += [
            pltpu.VMEM((width // LANES, act_rows, LANES), jnp.float32),
            pltpu.VMEM((own, LANES), jnp.float32),
            pltpu.VMEM((out_rows, LANES), jnp.float32),
            pltpu.VMEM((taps_n, width), z.dtype),
            pltpu.SemaphoreType.DMA((1,)),
        ]
        shapes += [
            jax.ShapeDtypeStruct((out_rows, width), jnp.bfloat16),
            jax.ShapeDtypeStruct((copies, 2, width), jnp.float32),
        ]
    plan = (
        do_mm, do_conv, layer, act_rows, own, layer * rim, chunks, group_at, taps_n, blocks
    )
    return pl.pallas_call(
        functools.partial(module_kernel, plan),
        out_shape=shapes,
        in_specs=specs,
        out_specs=[vmem] * len(shapes),
        scratch_shapes=scratch,
        compiler_params=pltpu.CompilerParams(vmem_limit_bytes=47 << 20),
        name="module_step",
    )(*args)


STAGES = ((0, 4), (4, 8))


def shards(frames_in, lengths, depth_kernel, batch_gain, batch_bias, out_weight):
    layer_total = lax.axis_size("segment")
    ctx_count = lax.axis_size("ctx")
    segment_index = lax.axis_index("segment")
    ctx_index = lax.axis_index("ctx")
    dp_index = lax.axis_index("dp")
    frames_dev = frames_in.shape[2]
    kernel_size = depth_kernel.shape[1]
    rim = kernel_size // 2
    both = [(0, 1), (1, 0)]
    forward = [(i, i + 1) for i in range(ctx_count - 1)]
    backward = [(b, a) for a, b in forward]

    half_rows = out_weight.shape[1] // 2
    mine = lax.dynamic_slice_in_dim(out_weight[0], dp_index * half_rows, half_rows, 0)
    scales = jnp.concatenate([batch_gain, batch_bias], axis=0)
    upper = lax.reduce_precision(scales, 8, 7)
    scales = jnp.stack([upper, scales - upper], axis=1).reshape(-1, scales.shape[1])
    z = jnp.concatenate(
        [
            mine,
            depth_kernel[0].astype(jnp.bfloat16),
            scales.astype(jnp.bfloat16),
            jnp.zeros((EXTRA - scales.shape[0], scales.shape[1]), jnp.bfloat16),
        ],
        axis=0,
    )
    z = lax.all_gather(z, "segment", axis=0)

    mine_len = lax.dynamic_slice_in_dim(lengths[0], segment_index, 1, 0)
    count = mine_len + lax.ppermute(mine_len, "dp", both)
    halo = rim * layer_total
    first = (ctx_index * frames_dev - halo).astype(jnp.int32)
    scal = jnp.concatenate([mine_len, first[None], count])

    own = lax.dynamic_index_in_dim(frames_in[0], segment_index, 0, keepdims=False)
    low = lax.ppermute(own[frames_dev - halo :], "ctx", forward)
    high = lax.ppermute(own[:halo], "ctx", backward)
    state = jnp.concatenate([low, own, high], axis=0)

    z, state = lax.optimization_barrier((z, state))
    rows = z[:, :half_rows]
    weights = {}
    for lo, hi in STAGES:
        parts = [lax.all_gather(rows[lo:hi], ("ctx", "dp"), axis=0)]
        for layer in range(lo, hi):
            weights[layer] = (parts, layer - lo)

    prev = None
    for layer in range(layer_total):
        state, mixed, sums = run_module(
            scal, state, z, frames_dev, layer, rim, ctx_count, prev, True
        )
        sums = lax.all_to_all(sums, "ctx", 0, 0, tiled=True)
        others = lax.ppermute(sums, "dp", both)
        prev = (mixed, sums, others, *weights[layer])
    (state,) = run_module(scal, state, z, frames_dev, layer_total, rim, ctx_count, prev, False)
    return state[None, None]


def solution(mesh):
    placed = (
        P("dp", None, "ctx", None),
        P("dp", None),
        P("segment", None, None),
        P("segment", None),
        P("segment", None),
        P("segment", "ctx", None),
    )
    return jax.shard_map(
        shards,
        mesh=mesh,
        in_specs=placed,
        out_specs=P("dp", "segment", "ctx", None),
        check_vma=False,
    )
```

```python
import functools

import jax
import jax.numpy as jnp
from jax import lax
from jax.experimental import pallas as pl
from jax.experimental.pallas import tpu as pltpu
from jax.sharding import PartitionSpec as P

EPSILON = 1e-05
LANES = 128
SUBLANES = 8
EXTRA = 8


def module_kernel(plan, *refs):
    do_mm, do_conv, layer, act_rows, own, first_at, chunks, group_at, taps_n, blocks = plan
    refs = list(refs)
    scal = refs.pop(0)
    if do_mm:
        mixed, sums, others = [refs.pop(0) for _ in range(3)]
        w_parts = [refs.pop(0) for _ in range(max(1, len(blocks)))]
    state, z_hbm = refs.pop(0), refs.pop(0)
    state_out = refs.pop(0)
    if do_conv:
        mixed_out, sums_out = refs.pop(0), refs.pop(0)
    if do_mm:
        act_s, w_s, sems, gb, gb_sem, affine = [refs.pop(0) for _ in range(6)]
        at = z_hbm.shape[1] - EXTRA
        gb_copy = pltpu.make_async_copy(z_hbm.at[layer - 1, pl.ds(at, EXTRA)], gb, gb_sem.at[0])
        gb_copy.start()
    if do_conv:
        norm_s, mask_s, mix_s, taps, tap_sem = [refs.pop(0) for _ in range(5)]
        at = z_hbm.shape[1] - EXTRA - taps_n
        tap_copy = pltpu.make_async_copy(z_hbm.at[layer, pl.ds(at, taps_n)], taps, tap_sem.at[0])
        tap_copy.start()

    width = state.shape[1]
    length = scal[0]
    first = scal[1] + first_at
    lane_groups = width // LANES

    def row_valid(row, rows, lanes):
        at = lax.broadcasted_iota(jnp.int32, (rows, lanes), 0) + (first + row)
        return jnp.where((at >= 0) & (at < length), 1.0, 0.0).astype(jnp.float32)

    if do_mm:
        wide = width // chunks
        copies = []
        if blocks:
            for part, count in zip(w_parts, blocks):
                for i in range(count):
                    n = len(copies)
                    copies.append(
                        pltpu.make_async_copy(
                            part.at[i, group_at], w_s.at[scal[3 + n]], sems.at[n]
                        )
                    )
        else:
            for n in range(chunks):
                lanes = pl.ds(n * wide, wide)
                copies.append(
                    pltpu.make_async_copy(
                        w_parts[0].at[:, group_at, :, lanes], w_s.at[:, :, lanes], sems.at[n]
                    )
                )
        for copy in copies:
            copy.start()
        total = sums[0] + others[0]
        for s in range(1, sums.shape[0]):
            total = total + sums[s] + others[s]
        count = scal[2].astype(jnp.float32)
        mean = total[0:1] / count
        var = total[1:2] / count - mean * mean
        gb_copy.wait()
        halves = gb[...].astype(jnp.float32)
        scale = lax.rsqrt(var + EPSILON) * (halves[0:1] + halves[1:2])
        shift = (halves[2:3] + halves[3:4]) - mean * scale
        affine[0:1, :] = 0.5 * scale
        affine[1:2, :] = 0.5 * shift
        valid = row_valid(0, act_rows, LANES)

        def activate(g, carry):
            lanes = pl.ds(pl.multiple_of(g * LANES, LANES), LANES)
            half = mixed[:, lanes].astype(jnp.float32) * affine[0:1, lanes] + affine[1:2, lanes]
            act = (half + half * jnp.tanh(half)) * valid
            act_s[:, lanes] = act.astype(jnp.bfloat16)
            return carry

        lax.fori_loop(0, lane_groups, activate, 0)
        top = (state.shape[0] - act_rows) // 2
        if blocks:
            for copy in copies:
                copy.wait()
        for n in range(chunks):
            lanes = slice(n * wide, (n + 1) * wide)
            if not blocks:
                copies[n].wait()
            rows = w_s[:, :, lanes].reshape(width, wide)
            product = jnp.dot(act_s[...], rows, preferred_element_type=jnp.float32)
            old = state[top : top + act_rows, lanes].astype(jnp.float32)
            state_out[:, lanes] = (old + product).astype(jnp.bfloat16)
        normed_from = state_out
    else:
        state_out[...] = state[...]
        normed_from = state

    if do_conv:
        block = 32

        def norm_rows(i, carry):
            row = pl.multiple_of(i * block, block)
            x = normed_from[pl.ds(row, block), :].astype(jnp.float32)
            mean = jnp.mean(x, axis=1, keepdims=True)
            x = x - mean
            var = jnp.mean(x * x, axis=1, keepdims=True)
            y = x * (lax.rsqrt(var + EPSILON) * row_valid(row, block, 1))
            y = y.astype(jnp.bfloat16).astype(jnp.float32)
            for g in range(lane_groups):
                norm_s[g, pl.ds(row, block), :] = y[:, g * LANES : (g + 1) * LANES]
            return carry

        lax.fori_loop(0, act_rows // block, norm_rows, 0)
        tap_copy.wait()
        out_rows = act_rows - taps_n
        edge = (out_rows - own) // 2
        mask_s[...] = row_valid(edge + taps_n // 2, own, LANES)
        tiles = out_rows // SUBLANES
        splits, run = conv_split(out_rows)

        def conv_lanes(g, carry):
            lanes = pl.ds(pl.multiple_of(g * LANES, LANES), LANES)
            for b in range(splits):
                base = b * (tiles // splits) * SUBLANES
                tap = [
                    jnp.broadcast_to(taps[k : k + 1, lanes].astype(jnp.float32), (SUBLANES, LANES))
                    for k in range(taps_n)
                ]
                acc = [None] * run
                for m in range(run + taps_n - 1):
                    v = norm_s[g, pl.ds(base + m, SUBLANES, stride=run), :]
                    for j in range(run):
                        if 0 <= m - j < taps_n:
                            term = tap[m - j] * v
                            acc[j] = term if acc[j] is None else acc[j] + term
                for j in range(run):
                    mix_s[pl.ds(base + j, SUBLANES, stride=run), :] = acc[j]
            mixed_out[:, lanes] = mix_s[:out_rows, :].astype(jnp.bfloat16)
            mine = mix_s[edge : edge + own, :]
            masked = mine * mask_s[...]
            one = jnp.sum(masked, axis=0, keepdims=True)
            two = jnp.sum(masked * mine, axis=0, keepdims=True)
            both = jnp.concatenate([one, two], axis=0)
            for c in range(sums_out.shape[0]):
                sums_out[c, :, lanes] = both
            return carry

        lax.fori_loop(0, lane_groups, conv_lanes, 0)


def conv_split(out_rows):
    tiles = out_rows // SUBLANES
    splits = 1 if tiles <= 24 else 2
    run = tiles // splits
    return splits, run + (run % SUBLANES == 0)


def run_module(scal, state, z, own, layer, rim, copies, prev, do_conv):
    width = state.shape[1]
    chunks = 6
    taps_n = 2 * rim
    do_mm = prev is not None
    vmem = pl.BlockSpec(memory_space=pltpu.VMEM)
    hbm = pl.BlockSpec(memory_space=pltpu.HBM)
    anywhere = pl.BlockSpec(memory_space=pl.ANY)
    args, specs = [scal], [pl.BlockSpec(memory_space=pltpu.SMEM)]
    scratch = []
    group_at, blocks = 0, ()
    act_rows = state.shape[0]
    if do_mm:
        mixed, sums, others, parts, group_at = prev
        act_rows = mixed.shape[0]
        args += [mixed, sums, others, *parts]
        specs += [vmem] * 3 + [hbm if len(parts) == 1 else anywhere] * len(parts)
        rows = parts[0].shape[2]
        if len(parts) > 1:
            blocks = tuple(p.shape[0] for p in parts)
        scratch += [
            pltpu.VMEM((act_rows, width), jnp.bfloat16),
            pltpu.VMEM((width // rows, rows, width), jnp.bfloat16),
            pltpu.SemaphoreType.DMA((max(chunks, sum(blocks)),)),
            pltpu.VMEM((EXTRA, width), z.dtype),
            pltpu.SemaphoreType.DMA((1,)),
            pltpu.VMEM((2, width), jnp.float32),
        ]
    args += [state, z]
    specs += [vmem, hbm]
    shapes = [jax.ShapeDtypeStruct((act_rows, width), jnp.bfloat16)]
    if do_conv:
        out_rows = act_rows - taps_n
        splits, run = conv_split(out_rows)
        more = SUBLANES * (run - out_rows // SUBLANES // splits)
        scratch += [
            pltpu.VMEM((width // LANES, act_rows + more, LANES), jnp.float32),
            pltpu.VMEM((own, LANES), jnp.float32),
            pltpu.VMEM((out_rows + more, LANES), jnp.float32),
            pltpu.VMEM((taps_n, width), z.dtype),
            pltpu.SemaphoreType.DMA((1,)),
        ]
        shapes += [
            jax.ShapeDtypeStruct((out_rows, width), jnp.bfloat16),
            jax.ShapeDtypeStruct((copies, 2, width), jnp.float32),
        ]
    plan = (
        do_mm, do_conv, layer, act_rows, own, layer * rim, chunks, group_at, taps_n, blocks
    )
    args = [
        pltpu.with_memory_space_constraint(a, pltpu.HBM) if spec is hbm else a
        for a, spec in zip(args, specs)
    ]
    return pl.pallas_call(
        functools.partial(module_kernel, plan),
        out_shape=shapes,
        in_specs=specs,
        out_specs=[vmem] * len(shapes),
        scratch_shapes=scratch,
        compiler_params=pltpu.CompilerParams(vmem_limit_bytes=32 << 20),
        name="module_step",
    )(*args)


SIDE = 4
STEPS = (0, 1, 3, 2)


def line_shift(steps, turned):
    pairs = []
    for p in range(SIDE):
        for q in range(SIDE):
            for core in range(2):
                to = (p, (q + steps) % SIDE) if core != turned else ((p + steps) % SIDE, q)
                pairs.append(((p * SIDE + q) * 2 + core, (to[0] * SIDE + to[1]) * 2 + core))
    return pairs


def along(x, steps):
    return lax.ppermute(x, ("ctx", "dp"), line_shift(steps, 0))


def across(x, steps):
    return lax.ppermute(x, ("ctx", "dp"), line_shift(steps, 1))


def plane_places(ctx_index, dp_index):
    moved = jnp.tile(jnp.array(STEPS, jnp.int32), SIDE)
    turned = jnp.repeat(jnp.array(STEPS, jnp.int32), SIDE)
    x, y = ctx_index // SIDE, ctx_index % SIDE
    by_x = ((x - moved) % SIDE * SIDE + (y - turned) % SIDE) * 2
    by_y = ((x - turned) % SIDE * SIDE + (y - moved) % SIDE) * 2 + 1
    first = dp_index == 0
    return jnp.concatenate([jnp.where(first, by_x, by_y), jnp.where(first, by_y, by_x)])


STAGES = ((1, 4), (4, 8))


def shards(frames_in, lengths, depth_kernel, batch_gain, batch_bias, out_weight):
    layer_total = lax.axis_size("segment")
    ctx_count = lax.axis_size("ctx")
    segment_index = lax.axis_index("segment")
    ctx_index = lax.axis_index("ctx")
    dp_index = lax.axis_index("dp")
    frames_dev = frames_in.shape[2]
    kernel_size = depth_kernel.shape[1]
    rim = kernel_size // 2
    both = [(0, 1), (1, 0)]
    forward = [(i, i + 1) for i in range(ctx_count - 1)]
    backward = [(b, a) for a, b in forward]

    half_rows = out_weight.shape[1] // 2
    mine = lax.dynamic_slice_in_dim(out_weight[0], dp_index * half_rows, half_rows, 0)
    scales = jnp.concatenate([batch_gain, batch_bias], axis=0)
    upper = lax.reduce_precision(scales, 8, 7)
    scales = jnp.stack([upper, scales - upper], axis=1).reshape(-1, scales.shape[1])
    z = jnp.concatenate(
        [
            mine,
            depth_kernel[0].astype(jnp.bfloat16),
            scales.astype(jnp.bfloat16),
            jnp.zeros((EXTRA - scales.shape[0], scales.shape[1]), jnp.bfloat16),
        ],
        axis=0,
    )
    z = lax.all_gather(z, "segment", axis=0)

    mine_len = lax.dynamic_slice_in_dim(lengths[0], segment_index, 1, 0)
    count = mine_len + lax.ppermute(mine_len, "dp", both)
    halo = rim * layer_total
    first = (ctx_index * frames_dev - halo).astype(jnp.int32)
    scal = jnp.concatenate([mine_len, first[None], count, plane_places(ctx_index, dp_index)])

    own = lax.dynamic_index_in_dim(frames_in[0], segment_index, 0, keepdims=False)
    low = lax.ppermute(own[frames_dev - halo :], "ctx", forward)
    high = lax.ppermute(own[:halo], "ctx", backward)
    state = jnp.concatenate([low, own, high], axis=0)

    z, state, scal = lax.optimization_barrier((z, state, scal))
    rows = z[:, :half_rows]
    weights = {}
    for lo, hi in STAGES:
        parts = [lax.all_gather(rows[lo:hi], ("ctx", "dp"), axis=0)]
        for layer in range(lo, hi):
            weights[layer] = (parts, layer - lo)

    line = [rows[:1]] + [along(rows[:1], steps) for steps in STEPS[1:]]

    prev = None
    for layer in range(layer_total):
        state, mixed, sums = run_module(
            scal, state, z, frames_dev, layer, rim, ctx_count, prev, True
        )
        if layer == 0:
            line, sums = lax.optimization_barrier((line, sums))
            line, sums = lax.optimization_barrier((jnp.stack(line), sums))
            parts = [line] + [across(line, steps) for steps in STEPS[1:]]
        sums = lax.all_to_all(sums, "ctx", 0, 0, tiled=True)
        if layer == 0:
            parts, sums = lax.optimization_barrier((parts, sums))
            weights[0] = (parts + [lax.ppermute(p, "dp", both) for p in parts], 0)
        others = lax.ppermute(sums, "dp", both)
        prev = (mixed, sums, others, *weights[layer])
    (state,) = run_module(scal, state, z, frames_dev, layer_total, rim, ctx_count, prev, False)
    return state[None, None]


def solution(mesh):
    placed = (
        P("dp", None, "ctx", None),
        P("dp", None),
        P("segment", None, None),
        P("segment", None),
        P("segment", None),
        P("segment", "ctx", None),
    )
    return jax.shard_map(
        shards,
        mesh=mesh,
        in_specs=placed,
        out_specs=P("dp", "segment", "ctx", None),
        check_vma=False,
    )
```

```python
import functools

import jax
import jax.numpy as jnp
from jax import lax
from jax.experimental import pallas as pl
from jax.experimental.pallas import tpu as pltpu
from jax.sharding import PartitionSpec as P

EPSILON = 1e-05
LANES = 128
SUBLANES = 8
EXTRA = 8


def module_kernel(plan, *refs):
    do_mm, do_conv, layer, act_rows, own, first_at, chunks, group_at, taps_n, blocks, far = plan
    far_in, far_out = far
    refs = list(refs)
    scal = refs.pop(0)
    if do_mm:
        mixed, sums, others = [refs.pop(0) for _ in range(3)]
        w_parts = [refs.pop(0) for _ in range(max(1, len(blocks)))]
    state, ring, other = [refs.pop(0) for _ in range(3)]
    state_out = refs.pop(0)
    if do_conv:
        mixed_out, sums_out = refs.pop(0), refs.pop(0)
    if do_mm:
        act_s, w_s, sems, gb, affine = [refs.pop(0) for _ in range(5)]
    if do_conv:
        norm_s, mask_s, mix_s, taps = [refs.pop(0) for _ in range(4)]
    z_sems = refs.pop(0)
    if far_in:
        mixed_hbm, state_hbm = mixed, state
        mixed, state, in_sems = [refs.pop(0) for _ in range(3)]
        pull = [
            pltpu.make_async_copy(mixed_hbm, mixed, in_sems.at[0]),
            pltpu.make_async_copy(state_hbm, state, in_sems.at[1]),
        ]
        for copy in pull:
            copy.start()
    if far_out:
        mixed_hbm_out, state_hbm_out = mixed_out, state_out
        mixed_out, state_out, out_sems = [refs.pop(0) for _ in range(3)]

    slots = ring.shape[0]
    core = scal[4]
    half_taps = taps_n // 2
    rows_at = ring.shape[1] - half_taps - EXTRA

    def slot_of(module):
        return lax.rem(module - scal[3] + slots, slots)

    if do_mm:
        at = slot_of(layer - 1)
        gb_copies = [
            pltpu.make_async_copy(
                ring.at[at, pl.ds(rows_at + half_taps, EXTRA)], gb.at[core], z_sems.at[0]
            ),
            pltpu.make_async_copy(
                other.at[at, pl.ds(half_taps, EXTRA)], gb.at[1 - core], z_sems.at[1]
            ),
        ]
        for copy in gb_copies:
            copy.start()
    if do_conv:
        at = slot_of(layer)
        to = [pl.ds(pl.multiple_of(c * half_taps, half_taps), half_taps) for c in (core, 1 - core)]
        tap_copies = [
            pltpu.make_async_copy(
                ring.at[at, pl.ds(rows_at, half_taps)], taps.at[to[0]], z_sems.at[2]
            ),
            pltpu.make_async_copy(
                other.at[at, pl.ds(0, half_taps)], taps.at[to[1]], z_sems.at[3]
            ),
        ]
        for copy in tap_copies:
            copy.start()

    width = state.shape[1]
    length = scal[0]
    first = scal[1] + first_at
    lane_groups = width // LANES

    def row_valid(row, rows, lanes):
        at = lax.broadcasted_iota(jnp.int32, (rows, lanes), 0) + (first + row)
        return jnp.where((at >= 0) & (at < length), 1.0, 0.0).astype(jnp.float32)

    if do_mm:
        wide = width // chunks
        copies = []
        if blocks:
            for part, count in zip(w_parts, blocks):
                for i in range(count):
                    n = len(copies)
                    copies.append(
                        pltpu.make_async_copy(
                            part.at[i, group_at], w_s.at[scal[5 + n]], sems.at[n]
                        )
                    )

        def chunk_copy(n):
            lanes = pl.ds(pl.multiple_of(n * wide, wide), wide)
            return pltpu.make_async_copy(
                w_parts[0].at[:, group_at, :, lanes], w_s.at[:, :, lanes], sems.at[n]
            )

        if not blocks:
            copies = [chunk_copy(n) for n in range(chunks)]
        for copy in copies:
            copy.start()
        total = sums[0] + others[0]
        for s in range(1, sums.shape[0]):
            total = total + sums[s] + others[s]
        count = scal[2].astype(jnp.float32)
        mean = total[0:1] / count
        var = total[1:2] / count - mean * mean
        for copy in gb_copies:
            copy.wait()
        gain, bias = gb[0].astype(jnp.float32), gb[1].astype(jnp.float32)
        scale = lax.rsqrt(var + EPSILON) * (gain[0:1] + gain[1:2])
        shift = (bias[0:1] + bias[1:2]) - mean * scale
        affine[0:1, :] = 0.5 * scale
        affine[1:2, :] = 0.5 * shift
        valid = row_valid(0, act_rows, LANES)

        def activate(g, carry):
            lanes = pl.ds(pl.multiple_of(g * LANES, LANES), LANES)
            half = mixed[:, lanes].astype(jnp.float32) * affine[0:1, lanes] + affine[1:2, lanes]
            act = (half + half * jnp.tanh(half)) * valid
            act_s[:, lanes] = act.astype(jnp.bfloat16)
            return carry

        if far_in:
            pull[0].wait()
        lax.fori_loop(0, lane_groups, activate, 0)
        if far_in:
            pull[1].wait()
        top = (state.shape[0] - act_rows) // 2
        if blocks:
            for copy in copies:
                copy.wait()

        def multiply(n, carry):
            lanes = pl.ds(pl.multiple_of(n * wide, wide), wide)
            if not blocks:
                chunk_copy(n).wait()
            rows = w_s[:, :, lanes].reshape(width, wide)
            product = jnp.dot(act_s[...], rows, preferred_element_type=jnp.float32)
            old = state[top : top + act_rows, lanes].astype(jnp.float32)
            state_out[:, lanes] = (old + product).astype(jnp.bfloat16)
            return carry

        lax.fori_loop(0, chunks, multiply, 0)
        normed_from = state_out
        if far_out:
            push_state = pltpu.make_async_copy(state_out, state_hbm_out, out_sems.at[0])
            push_state.start()
    else:
        state_out[...] = state[...]
        normed_from = state

    if do_conv:
        block = 32

        def norm_rows(i, carry):
            row = pl.multiple_of(i * block, block)
            x = normed_from[pl.ds(row, block), :].astype(jnp.float32)
            mean = jnp.mean(x, axis=1, keepdims=True)
            x = x - mean
            var = jnp.mean(x * x, axis=1, keepdims=True)
            y = x * (lax.rsqrt(var + EPSILON) * row_valid(row, block, 1))
            y = y.astype(jnp.bfloat16).astype(jnp.float32)
            for g in range(lane_groups):
                norm_s[g, pl.ds(row, block), :] = y[:, g * LANES : (g + 1) * LANES]
            return carry

        lax.fori_loop(0, act_rows // block, norm_rows, 0)
        for copy in tap_copies:
            copy.wait()
        out_rows = act_rows - taps_n
        edge = (out_rows - own) // 2
        mask_s[...] = row_valid(edge + taps_n // 2, own, LANES)
        tiles = out_rows // SUBLANES
        splits, run = conv_split(out_rows)

        def conv_lanes(g, carry):
            lanes = pl.ds(pl.multiple_of(g * LANES, LANES), LANES)
            for b in range(splits):
                base = b * (tiles // splits) * SUBLANES
                tap = [
                    jnp.broadcast_to(taps[k : k + 1, lanes].astype(jnp.float32), (SUBLANES, LANES))
                    for k in range(taps_n)
                ]
                acc = [None] * run
                for m in range(run + taps_n - 1):
                    v = norm_s[g, pl.ds(base + m, SUBLANES, stride=run), :]
                    for j in range(run):
                        if 0 <= m - j < taps_n:
                            term = tap[m - j] * v
                            acc[j] = term if acc[j] is None else acc[j] + term
                for j in range(run):
                    mix_s[pl.ds(base + j, SUBLANES, stride=run), :] = acc[j]
            mixed_out[:, lanes] = mix_s[:out_rows, :].astype(jnp.bfloat16)
            if far_out:
                pltpu.make_async_copy(
                    mixed_out.at[:, lanes], mixed_hbm_out.at[:, lanes], out_sems.at[1]
                ).start()
            mine = mix_s[edge : edge + own, :]
            masked = mine * mask_s[...]
            one = jnp.sum(masked, axis=0, keepdims=True)
            two = jnp.sum(masked * mine, axis=0, keepdims=True)
            both = jnp.concatenate([one, two], axis=0)
            for c in range(sums_out.shape[0]):
                sums_out[c, :, lanes] = both
            return carry

        lax.fori_loop(0, lane_groups, conv_lanes, 0)
        if far_out:
            push_state.wait()
            pltpu.make_async_copy(mixed_out, mixed_hbm_out, out_sems.at[1]).wait()


def conv_split(out_rows):
    tiles = out_rows // SUBLANES
    splits = 1 if tiles <= 24 else 2
    run = tiles // splits
    return splits, run + (run % SUBLANES == 0)


def run_module(scal, state, z, own, layer, rim, copies, prev, do_conv, far):
    width = state.shape[1]
    chunks = 6
    taps_n = 2 * rim
    do_mm = prev is not None
    vmem = pl.BlockSpec(memory_space=pltpu.VMEM)
    hbm = pl.BlockSpec(memory_space=pltpu.HBM)
    args, specs = [scal], [pl.BlockSpec(memory_space=pltpu.SMEM)]
    scratch = []
    group_at, blocks = 0, ()
    act_rows = state.shape[0]
    if do_mm:
        mixed, sums, others, parts, group_at = prev
        act_rows = mixed.shape[0]
        args += [mixed, sums, others, *parts]
        specs += [hbm if far[0] else vmem] + [vmem] * 2 + [hbm] * len(parts)
        rows = parts[0].shape[2]
        if len(parts) > 1:
            blocks = tuple(p.shape[0] for p in parts)
        scratch += [
            pltpu.VMEM((act_rows, width), jnp.bfloat16),
            pltpu.VMEM((width // rows, rows, width), jnp.bfloat16),
            pltpu.SemaphoreType.DMA((max(chunks, sum(blocks)),)),
            pltpu.VMEM((2, EXTRA, width), jnp.bfloat16),
            pltpu.VMEM((2, width), jnp.float32),
        ]
    args += [state, *z]
    specs += [hbm if far[0] else vmem, hbm, hbm]
    shapes = [jax.ShapeDtypeStruct((act_rows, width), jnp.bfloat16)]
    if do_conv:
        out_rows = act_rows - taps_n
        splits, run = conv_split(out_rows)
        more = SUBLANES * (run - out_rows // SUBLANES // splits)
        scratch += [
            pltpu.VMEM((width // LANES, act_rows + more, LANES), jnp.float32),
            pltpu.VMEM((own, LANES), jnp.float32),
            pltpu.VMEM((out_rows + more, LANES), jnp.float32),
            pltpu.VMEM((taps_n, width), jnp.bfloat16),
        ]
        shapes += [
            jax.ShapeDtypeStruct((out_rows, width), jnp.bfloat16),
            jax.ShapeDtypeStruct((copies, 2, width), jnp.float32),
        ]
    out_specs = [vmem] * len(shapes)
    scratch.append(pltpu.SemaphoreType.DMA((4,)))
    if far[0]:
        scratch += [
            pltpu.VMEM(mixed.shape, mixed.dtype),
            pltpu.VMEM(state.shape, state.dtype),
            pltpu.SemaphoreType.DMA((2,)),
        ]
    if far[1]:
        out_specs[0] = out_specs[1] = hbm
        scratch += [
            pltpu.VMEM(shapes[1].shape, shapes[1].dtype),
            pltpu.VMEM(shapes[0].shape, shapes[0].dtype),
            pltpu.SemaphoreType.DMA((2,)),
        ]
    plan = (
        do_mm, do_conv, layer, act_rows, own, layer * rim, chunks, group_at, taps_n, blocks, far
    )
    args = [
        pltpu.with_memory_space_constraint(a, pltpu.HBM) if spec is hbm else a
        for a, spec in zip(args, specs)
    ]
    return pl.pallas_call(
        functools.partial(module_kernel, plan),
        out_shape=shapes,
        in_specs=specs,
        out_specs=out_specs,
        scratch_shapes=scratch,
        compiler_params=pltpu.CompilerParams(vmem_limit_bytes=32 << 20),
        name="module_step",
    )(*args)


SIDE = 4
STEPS = (0, 1, 3, 2)


def line_shift(steps, turned):
    pairs = []
    for p in range(SIDE):
        for q in range(SIDE):
            for core in range(2):
                to = (p, (q + steps) % SIDE) if core != turned else ((p + steps) % SIDE, q)
                pairs.append(((p * SIDE + q) * 2 + core, (to[0] * SIDE + to[1]) * 2 + core))
    return pairs


def along(x, steps):
    return lax.ppermute(x, ("ctx", "dp"), line_shift(steps, 0))


def across(x, steps):
    return lax.ppermute(x, ("ctx", "dp"), line_shift(steps, 1))


def plane_places(ctx_index, dp_index):
    moved = jnp.tile(jnp.array(STEPS, jnp.int32), SIDE)
    turned = jnp.repeat(jnp.array(STEPS, jnp.int32), SIDE)
    x, y = ctx_index // SIDE, ctx_index % SIDE
    by_x = ((x - moved) % SIDE * SIDE + (y - turned) % SIDE) * 2
    by_y = ((x - turned) % SIDE * SIDE + (y - moved) % SIDE) * 2 + 1
    first = dp_index == 0
    return jnp.concatenate([jnp.where(first, by_x, by_y), jnp.where(first, by_y, by_x)])


STAGES = ((1, 4), (4, 8))


def shards(frames_in, lengths, depth_kernel, batch_gain, batch_bias, out_weight):
    layer_total = lax.axis_size("segment")
    ctx_count = lax.axis_size("ctx")
    segment_index = lax.axis_index("segment")
    ctx_index = lax.axis_index("ctx")
    dp_index = lax.axis_index("dp")
    frames_dev = frames_in.shape[2]
    kernel_size = depth_kernel.shape[1]
    rim = kernel_size // 2
    both = [(0, 1), (1, 0)]
    forward = [(i, i + 1) for i in range(ctx_count - 1)]
    backward = [(b, a) for a, b in forward]

    half_rows = out_weight.shape[1] // 2
    mine = lax.dynamic_slice_in_dim(out_weight[0], dp_index * half_rows, half_rows, 0)
    scales = jnp.where(dp_index == 0, batch_gain, batch_bias)
    upper = lax.reduce_precision(scales, 8, 7)
    scales = jnp.concatenate([upper, scales - upper], axis=0).astype(jnp.bfloat16)
    mine_taps = lax.dynamic_slice_in_dim(depth_kernel[0], dp_index * rim, rim, 0)
    pad = jnp.zeros((EXTRA - scales.shape[0], scales.shape[1]), jnp.bfloat16)
    mine = jnp.concatenate([mine, mine_taps.astype(jnp.bfloat16), scales, pad], axis=0)

    def shift(x, steps):
        pairs = [(i, (i + steps) % layer_total) for i in range(layer_total)]
        return lax.ppermute(x, "segment", pairs)

    up, down = [mine], [mine]
    for _ in range(layer_total // 2 - 1):
        up.append(shift(up[-1], 1))
        down.append(shift(down[-1], -1))
    facing = [shift(up[-1][:half_rows], 1), shift(down[-1][half_rows:], -1)]
    ring = jnp.stack([*down, jnp.concatenate(facing, axis=0), *up[:0:-1]])

    mine_len = lax.dynamic_slice_in_dim(lengths[0], segment_index, 1, 0)
    count = mine_len + lax.ppermute(mine_len, "dp", both)
    halo = rim * layer_total
    first = (ctx_index * frames_dev - halo).astype(jnp.int32)
    scal = [mine_len, first[None], count, segment_index[None], dp_index[None]]
    scal = jnp.concatenate([*scal, plane_places(ctx_index, dp_index)])

    own = lax.dynamic_index_in_dim(frames_in[0], segment_index, 0, keepdims=False)
    low = lax.ppermute(own[frames_dev - halo :], "ctx", forward)
    high = lax.ppermute(own[:halo], "ctx", backward)
    state = jnp.concatenate([low, own, high], axis=0)

    ring, state, scal = lax.optimization_barrier((ring, state, scal))

    def rows_of(lo, hi):
        slots = [(layer - segment_index) % layer_total for layer in range(lo, hi)]
        size = (1, half_rows, ring.shape[2])
        return jnp.concatenate([lax.dynamic_slice(ring, (at, 0, 0), size) for at in slots])

    weights = {}
    for lo, hi in STAGES:
        parts = [lax.all_gather(rows_of(lo, hi), ("ctx", "dp"), axis=0)]
        for layer in range(lo, hi):
            weights[layer] = (parts, layer - lo)

    line = rows_of(0, 1)
    line = [line] + [along(line, steps) for steps in STEPS[1:]]
    z = (ring, lax.ppermute(ring[:, half_rows:], "dp", both))
    waits = [lo for lo, _ in STAGES]

    prev = None
    for layer in range(layer_total):
        far = (layer - 1 in waits, layer in waits)
        state, mixed, sums = run_module(
            scal, state, z, frames_dev, layer, rim, ctx_count, prev, True, far
        )
        if layer == 0:
            line, sums = lax.optimization_barrier((line, sums))
            line, sums = lax.optimization_barrier((jnp.stack(line), sums))
            parts = [line] + [across(line, steps) for steps in STEPS[1:]]
        sums = lax.all_to_all(sums, "ctx", 0, 0, tiled=True)
        if layer == 0:
            parts, sums = lax.optimization_barrier((parts, sums))
            weights[0] = (parts + [lax.ppermute(p, "dp", both) for p in parts], 0)
        others = lax.ppermute(sums, "dp", both)
        prev = (mixed, sums, others, *weights[layer])
    far = (False, False)
    (state,) = run_module(
        scal, state, z, frames_dev, layer_total, rim, ctx_count, prev, False, far
    )
    return state[None, None]


def solution(mesh):
    placed = (
        P("dp", None, "ctx", None),
        P("dp", None),
        P("segment", None, None),
        P("segment", None),
        P("segment", None),
        P("segment", "ctx", None),
    )
    return jax.shard_map(
        shards,
        mesh=mesh,
        in_specs=placed,
        out_specs=P("dp", "segment", "ctx", None),
        check_vma=False,
    )
```

```python
import functools

import jax
import jax.numpy as jnp
from jax import lax
from jax.experimental import pallas as pl
from jax.experimental.pallas import tpu as pltpu
from jax.sharding import PartitionSpec as P

EPSILON = 1e-05
LANES = 128
SUBLANES = 8
EXTRA = 8


def module_kernel(plan, *refs):
    do_mm, do_conv, layer, act_rows, own, first_at, chunks, group_at, taps_n, blocks, far, fetch = plan
    far_in, far_out = far
    held, next_at = fetch
    refs = list(refs)
    scal = refs.pop(0)
    if do_mm:
        mixed, sums, others = [refs.pop(0) for _ in range(3)]
        w_parts = [refs.pop(0) for _ in range(max(1, len(blocks)))]
    state, ring, other = [refs.pop(0) for _ in range(3)]
    next_hbm = refs.pop(0) if next_at is not None else None
    state_out = refs.pop(0)
    if do_conv:
        mixed_out, sums_out = refs.pop(0), refs.pop(0)
    w_next = refs.pop(0) if next_at is not None else None
    if do_mm:
        act_s, gb, affine = [refs.pop(0) for _ in range(3)]
        w_s, sems = (w_parts[0], None) if held else (refs.pop(0), refs.pop(0))
    if do_conv:
        norm_s, mask_s, mix_s, taps = [refs.pop(0) for _ in range(4)]
    z_sems = refs.pop(0)
    if next_at is not None:
        next_copy = pltpu.make_async_copy(next_hbm.at[:, next_at], w_next, z_sems.at[4])
    if far_in:
        mixed_hbm, state_hbm = mixed, state
        mixed, state, in_sems = [refs.pop(0) for _ in range(3)]
        pull = [
            pltpu.make_async_copy(mixed_hbm, mixed, in_sems.at[0]),
            pltpu.make_async_copy(state_hbm, state, in_sems.at[1]),
        ]
        for copy in pull:
            copy.start()
    if far_out:
        mixed_hbm_out, state_hbm_out = mixed_out, state_out
        mixed_out, state_out, out_sems = [refs.pop(0) for _ in range(3)]

    slots = ring.shape[0]
    core = scal[4]
    half_taps = taps_n // 2
    rows_at = ring.shape[1] - half_taps - EXTRA

    def slot_of(module):
        return lax.rem(module - scal[3] + slots, slots)

    if do_mm:
        at = slot_of(layer - 1)
        gb_copies = [
            pltpu.make_async_copy(
                ring.at[at, pl.ds(rows_at + half_taps, EXTRA)], gb.at[core], z_sems.at[0]
            ),
            pltpu.make_async_copy(
                other.at[at, pl.ds(half_taps, EXTRA)], gb.at[1 - core], z_sems.at[1]
            ),
        ]
        for copy in gb_copies:
            copy.start()
    if do_conv:
        at = slot_of(layer)
        to = [pl.ds(pl.multiple_of(c * half_taps, half_taps), half_taps) for c in (core, 1 - core)]
        tap_copies = [
            pltpu.make_async_copy(
                ring.at[at, pl.ds(rows_at, half_taps)], taps.at[to[0]], z_sems.at[2]
            ),
            pltpu.make_async_copy(
                other.at[at, pl.ds(0, half_taps)], taps.at[to[1]], z_sems.at[3]
            ),
        ]
        for copy in tap_copies:
            copy.start()

    width = state.shape[1]
    length = scal[0]
    first = scal[1] + first_at
    lane_groups = width // LANES

    def row_valid(row, rows, lanes):
        at = lax.broadcasted_iota(jnp.int32, (rows, lanes), 0) + (first + row)
        return jnp.where((at >= 0) & (at < length), 1.0, 0.0).astype(jnp.float32)

    if do_mm:
        wide = width // chunks
        copies = []
        if blocks:
            for part, count in zip(w_parts, blocks):
                for i in range(count):
                    n = len(copies)
                    copies.append(
                        pltpu.make_async_copy(
                            part.at[i, group_at], w_s.at[scal[5 + n]], sems.at[n]
                        )
                    )

        def chunk_copy(n):
            lanes = pl.ds(pl.multiple_of(n * wide, wide), wide)
            return pltpu.make_async_copy(
                w_parts[0].at[:, group_at, :, lanes], w_s.at[:, :, lanes], sems.at[n]
            )

        if not blocks and not held:
            copies = [chunk_copy(n) for n in range(chunks)]
        for copy in copies:
            copy.start()
        total = sums[0] + others[0]
        for s in range(1, sums.shape[0]):
            total = total + sums[s] + others[s]
        count = scal[2].astype(jnp.float32)
        mean = total[0:1] / count
        var = total[1:2] / count - mean * mean
        for copy in gb_copies:
            copy.wait()
        gain, bias = gb[0].astype(jnp.float32), gb[1].astype(jnp.float32)
        scale = lax.rsqrt(var + EPSILON) * (gain[0:1] + gain[1:2])
        shift = (bias[0:1] + bias[1:2]) - mean * scale
        affine[0:1, :] = 0.5 * scale
        affine[1:2, :] = 0.5 * shift
        valid = row_valid(0, act_rows, LANES)

        def activate(g, carry):
            lanes = pl.ds(pl.multiple_of(g * LANES, LANES), LANES)
            half = mixed[:, lanes].astype(jnp.float32) * affine[0:1, lanes] + affine[1:2, lanes]
            act = (half + half * jnp.tanh(half)) * valid
            act_s[:, lanes] = act.astype(jnp.bfloat16)
            return carry

        if far_in:
            pull[0].wait()
        lax.fori_loop(0, lane_groups, activate, 0)
        if far_in:
            pull[1].wait()
        top = (state.shape[0] - act_rows) // 2
        if blocks:
            for copy in copies:
                copy.wait()

        def multiply(n, carry):
            lanes = pl.ds(pl.multiple_of(n * wide, wide), wide)
            if not blocks and not held:
                chunk_copy(n).wait()
            rows = w_s[:, :, lanes].reshape(width, wide)
            product = jnp.dot(act_s[...], rows, preferred_element_type=jnp.float32)
            old = state[top : top + act_rows, lanes].astype(jnp.float32)
            state_out[:, lanes] = (old + product).astype(jnp.bfloat16)
            return carry

        lax.fori_loop(0, chunks, multiply, 0)
        if next_at is not None:
            next_copy.start()
        normed_from = state_out
        if far_out:
            push_state = pltpu.make_async_copy(state_out, state_hbm_out, out_sems.at[0])
            push_state.start()
    else:
        state_out[...] = state[...]
        normed_from = state

    if do_conv:
        block = 32

        def norm_rows(i, carry):
            row = pl.multiple_of(i * block, block)
            x = normed_from[pl.ds(row, block), :].astype(jnp.float32)
            mean = jnp.mean(x, axis=1, keepdims=True)
            x = x - mean
            var = jnp.mean(x * x, axis=1, keepdims=True)
            y = x * (lax.rsqrt(var + EPSILON) * row_valid(row, block, 1))
            y = y.astype(jnp.bfloat16).astype(jnp.float32)
            for g in range(lane_groups):
                norm_s[g, pl.ds(row, block), :] = y[:, g * LANES : (g + 1) * LANES]
            return carry

        lax.fori_loop(0, act_rows // block, norm_rows, 0)
        for copy in tap_copies:
            copy.wait()
        out_rows = act_rows - taps_n
        edge = (out_rows - own) // 2
        mask_s[...] = row_valid(edge + taps_n // 2, own, LANES)
        tiles = out_rows // SUBLANES
        splits, run = conv_split(out_rows)

        def conv_lanes(g, carry):
            lanes = pl.ds(pl.multiple_of(g * LANES, LANES), LANES)
            for b in range(splits):
                base = b * (tiles // splits) * SUBLANES
                tap = [
                    jnp.broadcast_to(taps[k : k + 1, lanes].astype(jnp.float32), (SUBLANES, LANES))
                    for k in range(taps_n)
                ]
                acc = [None] * run
                for m in range(run + taps_n - 1):
                    v = norm_s[g, pl.ds(base + m, SUBLANES, stride=run), :]
                    for j in range(run):
                        if 0 <= m - j < taps_n:
                            term = tap[m - j] * v
                            acc[j] = term if acc[j] is None else acc[j] + term
                for j in range(run):
                    mix_s[pl.ds(base + j, SUBLANES, stride=run), :] = acc[j]
            mixed_out[:, lanes] = mix_s[:out_rows, :].astype(jnp.bfloat16)
            if far_out:
                pltpu.make_async_copy(
                    mixed_out.at[:, lanes], mixed_hbm_out.at[:, lanes], out_sems.at[1]
                ).start()
            mine = mix_s[edge : edge + own, :]
            masked = mine * mask_s[...]
            one = jnp.sum(masked, axis=0, keepdims=True)
            two = jnp.sum(masked * mine, axis=0, keepdims=True)
            both = jnp.concatenate([one, two], axis=0)
            for c in range(sums_out.shape[0]):
                sums_out[c, :, lanes] = both
            return carry

        lax.fori_loop(0, lane_groups, conv_lanes, 0)
        if next_at is not None:
            next_copy.wait()
        if far_out:
            push_state.wait()
            pltpu.make_async_copy(mixed_out, mixed_hbm_out, out_sems.at[1]).wait()


def conv_split(out_rows):
    tiles = out_rows // SUBLANES
    splits = 1 if tiles <= 24 else 2
    run = tiles // splits
    return splits, run + (run % SUBLANES == 0)


def run_module(scal, state, z, own, layer, rim, copies, prev, do_conv, far, coming=None):
    width = state.shape[1]
    chunks = 6
    taps_n = 2 * rim
    do_mm = prev is not None
    vmem = pl.BlockSpec(memory_space=pltpu.VMEM)
    hbm = pl.BlockSpec(memory_space=pltpu.HBM)
    args, specs = [scal], [pl.BlockSpec(memory_space=pltpu.SMEM)]
    scratch = []
    group_at, blocks, held = 0, (), False
    act_rows = state.shape[0]
    if do_mm:
        mixed, sums, others, parts, group_at = prev
        act_rows = mixed.shape[0]
        args += [mixed, sums, others, *parts]
        held = group_at is None
        specs += [hbm if far[0] else vmem] + [vmem] * 2 + [vmem if held else hbm] * len(parts)
        rows = parts[0].shape[-2]
        if len(parts) > 1:
            blocks = tuple(p.shape[0] for p in parts)
        scratch += [
            pltpu.VMEM((act_rows, width), jnp.bfloat16),
            pltpu.VMEM((2, EXTRA, width), jnp.bfloat16),
            pltpu.VMEM((2, width), jnp.float32),
        ]
        if not held:
            scratch += [
                pltpu.VMEM((width // rows, rows, width), jnp.bfloat16),
                pltpu.SemaphoreType.DMA((max(chunks, sum(blocks)),)),
            ]
    args += [state, *z]
    specs += [hbm if far[0] else vmem, hbm, hbm]
    if coming is not None:
        args.append(coming[0])
        specs.append(hbm)
    shapes = [jax.ShapeDtypeStruct((act_rows, width), jnp.bfloat16)]
    if do_conv:
        out_rows = act_rows - taps_n
        splits, run = conv_split(out_rows)
        more = SUBLANES * (run - out_rows // SUBLANES // splits)
        scratch += [
            pltpu.VMEM((width // LANES, act_rows + more, LANES), jnp.float32),
            pltpu.VMEM((own, LANES), jnp.float32),
            pltpu.VMEM((out_rows + more, LANES), jnp.float32),
            pltpu.VMEM((taps_n, width), jnp.bfloat16),
        ]
        shapes += [
            jax.ShapeDtypeStruct((out_rows, width), jnp.bfloat16),
            jax.ShapeDtypeStruct((copies, 2, width), jnp.float32),
        ]
    if coming is not None:
        blocks_n, _, rows, _ = coming[0].shape
        shapes.append(jax.ShapeDtypeStruct((blocks_n, rows, width), jnp.bfloat16))
    out_specs = [vmem] * len(shapes)
    scratch.append(pltpu.SemaphoreType.DMA((5,)))
    if far[0]:
        scratch += [
            pltpu.VMEM(mixed.shape, mixed.dtype),
            pltpu.VMEM(state.shape, state.dtype),
            pltpu.SemaphoreType.DMA((2,)),
        ]
    if far[1]:
        out_specs[0] = out_specs[1] = hbm
        shapes = [pltpu.HBM(a.shape, a.dtype) for a in shapes[:2]] + shapes[2:]
        scratch += [
            pltpu.VMEM(shapes[1].shape, shapes[1].dtype),
            pltpu.VMEM(shapes[0].shape, shapes[0].dtype),
            pltpu.SemaphoreType.DMA((2,)),
        ]
    plan = (
        do_mm, do_conv, layer, act_rows, own, layer * rim, chunks, group_at, taps_n, blocks, far,
        (held, None if coming is None else coming[1]),
    )
    args = [
        pltpu.with_memory_space_constraint(a, pltpu.HBM) if spec is hbm else a
        for a, spec in zip(args, specs)
    ]
    return pl.pallas_call(
        functools.partial(module_kernel, plan),
        out_shape=shapes,
        in_specs=specs,
        out_specs=out_specs,
        scratch_shapes=scratch,
        compiler_params=pltpu.CompilerParams(vmem_limit_bytes=32 << 20),
        name="module_step",
    )(*args)


SIDE = 4
STEPS = (0, 1, 3, 2)


def line_shift(steps, turned):
    pairs = []
    for p in range(SIDE):
        for q in range(SIDE):
            for core in range(2):
                to = (p, (q + steps) % SIDE) if core != turned else ((p + steps) % SIDE, q)
                pairs.append(((p * SIDE + q) * 2 + core, (to[0] * SIDE + to[1]) * 2 + core))
    return pairs


def along(x, steps):
    return lax.ppermute(x, ("ctx", "dp"), line_shift(steps, 0))


def across(x, steps):
    return lax.ppermute(x, ("ctx", "dp"), line_shift(steps, 1))


def plane_places():
    places = []
    for x in range(SIDE):
        for y in range(SIDE):
            by_core = [
                [((x - p) % SIDE * SIDE + (y - q) % SIDE) * 2 for q in STEPS for p in STEPS],
                [((x - q) % SIDE * SIDE + (y - p) % SIDE) * 2 + 1 for q in STEPS for p in STEPS],
            ]
            places += [by_core[0] + by_core[1], by_core[1] + by_core[0]]
    return jnp.array(places, jnp.int32)


STAGES = ((1, 4), (4, 8))


def shards(frames_in, lengths, depth_kernel, batch_gain, batch_bias, out_weight):
    layer_total = lax.axis_size("segment")
    ctx_count = lax.axis_size("ctx")
    segment_index = lax.axis_index("segment")
    ctx_index = lax.axis_index("ctx")
    dp_index = lax.axis_index("dp")
    frames_dev = frames_in.shape[2]
    kernel_size = depth_kernel.shape[1]
    rim = kernel_size // 2
    both = [(0, 1), (1, 0)]
    forward = [(i, i + 1) for i in range(ctx_count - 1)]
    backward = [(b, a) for a, b in forward]

    half_rows = out_weight.shape[1] // 2
    mine = lax.dynamic_slice_in_dim(out_weight[0], dp_index * half_rows, half_rows, 0)
    scales = jnp.where(dp_index == 0, batch_gain, batch_bias)
    upper = lax.reduce_precision(scales, 8, 7)
    scales = jnp.concatenate([upper, scales - upper], axis=0).astype(jnp.bfloat16)
    mine_taps = lax.dynamic_slice_in_dim(depth_kernel[0], dp_index * rim, rim, 0)
    pad = jnp.zeros((EXTRA - scales.shape[0], scales.shape[1]), jnp.bfloat16)
    mine = jnp.concatenate([mine, mine_taps.astype(jnp.bfloat16), scales, pad], axis=0)

    def shift(x, steps):
        pairs = [(i, (i + steps) % layer_total) for i in range(layer_total)]
        return lax.ppermute(x, "segment", pairs)

    up, down = [mine], [mine]
    for _ in range(2):
        up.append(shift(up[-1], 1))
        down.append(shift(down[-1], -1))

    mine_len = lax.dynamic_slice_in_dim(lengths[0], segment_index, 1, 0)
    count = mine_len + lax.ppermute(mine_len, "dp", both)
    halo = rim * layer_total
    first = (ctx_index * frames_dev - halo).astype(jnp.int32)
    scal = [mine_len, first[None], count, segment_index[None], dp_index[None]]
    places = lax.dynamic_index_in_dim(plane_places(), ctx_index * 2 + dp_index, 0, keepdims=False)
    scal = jnp.concatenate([*scal, places])

    own = lax.dynamic_index_in_dim(frames_in[0], segment_index, 0, keepdims=False)
    own, up[2], down[2] = lax.optimization_barrier((own, up[2], down[2]))
    for _ in range(2, layer_total // 2 - 1):
        up.append(shift(up[-1], 1))
        down.append(shift(down[-1], -1))
    facing = [shift(up[-1][:half_rows], 1), shift(down[-1][half_rows:], -1)]
    ring = jnp.stack([*down, jnp.concatenate(facing, axis=0), *up[:0:-1]])

    low = lax.ppermute(own[frames_dev - halo :], "ctx", forward)
    high = lax.ppermute(own[:halo], "ctx", backward)
    state = jnp.concatenate([low, own, high], axis=0)

    ring, state, scal = lax.optimization_barrier((ring, state, scal))

    def rows_of(lo, hi):
        slots = [(layer - segment_index) % layer_total for layer in range(lo, hi)]
        size = (1, half_rows, ring.shape[2])
        return jnp.concatenate([lax.dynamic_slice(ring, (at, 0, 0), size) for at in slots])

    weights = {}
    for lo, hi in STAGES:
        parts = [lax.all_gather(rows_of(lo, hi), ("ctx", "dp"), axis=0)]
        for layer in range(lo, hi):
            weights[layer] = (parts, layer - lo)

    line = rows_of(0, 1)
    line = [line] + [along(line, steps) for steps in STEPS[1:]]
    z = (ring, lax.ppermute(ring[:, half_rows:], "dp", both))
    waits = [lo for lo, _ in STAGES]

    prev = None
    for layer in range(layer_total):
        far = (layer - 1 in waits, layer in waits)
        coming = None
        if layer > 1 and layer not in waits and layer - 1 in weights:
            parts, group_at = weights[layer]
            coming = (parts[0], group_at)
        state, mixed, sums, *fetched = run_module(
            scal, state, z, frames_dev, layer, rim, ctx_count, prev, True, far, coming
        )
        if layer == 0:
            line, sums = lax.optimization_barrier((line, sums))
            line, sums = lax.optimization_barrier((jnp.stack(line), sums))
            parts = [line] + [across(line, steps) for steps in STEPS[1:]]
        sums = lax.all_to_all(sums, "ctx", 0, 0, tiled=True)
        if layer == 0:
            parts, sums = lax.optimization_barrier((parts, sums))
            weights[0] = (parts + [lax.ppermute(p, "dp", both) for p in parts], 0)
        others = lax.ppermute(sums, "dp", both)
        prev = (mixed, sums, others, *((fetched, None) if fetched else weights[layer]))
    far = (False, False)
    (state,) = run_module(
        scal, state, z, frames_dev, layer_total, rim, ctx_count, prev, False, far
    )
    return state[None, None]


def solution(mesh):
    placed = (
        P("dp", None, "ctx", None),
        P("dp", None),
        P("segment", None, None),
        P("segment", None),
        P("segment", None),
        P("segment", "ctx", None),
    )
    return jax.shard_map(
        shards,
        mesh=mesh,
        in_specs=placed,
        out_specs=P("dp", "segment", "ctx", None),
        check_vma=False,
    )
```

```python
import functools

import jax
import jax.numpy as jnp
from jax import lax
from jax.experimental import pallas as pl
from jax.experimental.pallas import tpu as pltpu
from jax.sharding import PartitionSpec as P

EPSILON = 1e-05
LANES = 128
SUBLANES = 8
EXTRA = 8


def module_kernel(plan, *refs):
    do_mm, do_conv, layer, act_rows, own, first_at, chunks, group_at, taps_n, blocks, far = plan
    far_in, far_out = far
    refs = list(refs)
    scal = refs.pop(0)
    if do_mm:
        mixed, sums, others = [refs.pop(0) for _ in range(3)]
        w_parts = [refs.pop(0) for _ in range(max(1, len(blocks)))]
    state, ring, other = [refs.pop(0) for _ in range(3)]
    state_out = refs.pop(0)
    if do_conv:
        mixed_out, sums_out = refs.pop(0), refs.pop(0)
    if do_mm:
        act_s, w_s, sems, gb, affine = [refs.pop(0) for _ in range(5)]
    if do_conv:
        norm_s, mask_s, mix_s, taps = [refs.pop(0) for _ in range(4)]
    z_sems = refs.pop(0)
    if far_in:
        mixed_hbm, state_hbm = mixed, state
        mixed, state, in_sems = [refs.pop(0) for _ in range(3)]
        pull = [
            pltpu.make_async_copy(mixed_hbm, mixed, in_sems.at[0]),
            pltpu.make_async_copy(state_hbm, state, in_sems.at[1]),
        ]
        for copy in pull:
            copy.start()
    if far_out:
        mixed_hbm_out, state_hbm_out = mixed_out, state_out
        mixed_out, state_out, out_sems = [refs.pop(0) for _ in range(3)]

    core = scal[3]
    half_taps = taps_n // 2
    rows_at = ring.shape[1] - half_taps - EXTRA

    if do_mm:
        at = layer - 1
        gb_copies = [
            pltpu.make_async_copy(
                ring.at[at, pl.ds(rows_at + half_taps, EXTRA)], gb.at[core], z_sems.at[0]
            ),
            pltpu.make_async_copy(
                other.at[at, pl.ds(half_taps, EXTRA)], gb.at[1 - core], z_sems.at[1]
            ),
        ]
        for copy in gb_copies:
            copy.start()
    if do_conv:
        at = layer
        to = [pl.ds(pl.multiple_of(c * half_taps, half_taps), half_taps) for c in (core, 1 - core)]
        tap_copies = [
            pltpu.make_async_copy(
                ring.at[at, pl.ds(rows_at, half_taps)], taps.at[to[0]], z_sems.at[2]
            ),
            pltpu.make_async_copy(
                other.at[at, pl.ds(0, half_taps)], taps.at[to[1]], z_sems.at[3]
            ),
        ]
        for copy in tap_copies:
            copy.start()

    width = state.shape[1]
    length = scal[0]
    first = scal[1] + first_at
    lane_groups = width // LANES

    def row_valid(row, rows, lanes):
        at = lax.broadcasted_iota(jnp.int32, (rows, lanes), 0) + (first + row)
        return jnp.where((at >= 0) & (at < length), 1.0, 0.0).astype(jnp.float32)

    if do_mm:
        wide = width // chunks
        copies = []
        if blocks:
            for part, count in zip(w_parts, blocks):
                for i in range(count):
                    n = len(copies)
                    copies.append(
                        pltpu.make_async_copy(
                            part.at[i, group_at], w_s.at[scal[4 + n]], sems.at[n]
                        )
                    )

        def chunk_copy(n):
            lanes = pl.ds(pl.multiple_of(n * wide, wide), wide)
            return pltpu.make_async_copy(
                w_parts[0].at[:, group_at, :, lanes], w_s.at[:, :, lanes], sems.at[n]
            )

        if not blocks:
            copies = [chunk_copy(n) for n in range(chunks)]
        for copy in copies:
            copy.start()
        total = sums[0] + others[0]
        for s in range(1, sums.shape[0]):
            total = total + sums[s] + others[s]
        count = scal[2].astype(jnp.float32)
        mean = total[0:1] / count
        var = total[1:2] / count - mean * mean
        for copy in gb_copies:
            copy.wait()
        gain, bias = gb[0].astype(jnp.float32), gb[1].astype(jnp.float32)
        scale = lax.rsqrt(var + EPSILON) * (gain[0:1] + gain[1:2])
        shift = (bias[0:1] + bias[1:2]) - mean * scale
        affine[0:1, :] = 0.5 * scale
        affine[1:2, :] = 0.5 * shift
        valid = row_valid(0, act_rows, LANES)

        def activate(g, carry):
            lanes = pl.ds(pl.multiple_of(g * LANES, LANES), LANES)
            half = mixed[:, lanes].astype(jnp.float32) * affine[0:1, lanes] + affine[1:2, lanes]
            act = (half + half * jnp.tanh(half)) * valid
            act_s[:, lanes] = act.astype(jnp.bfloat16)
            return carry

        if far_in:
            pull[0].wait()
        lax.fori_loop(0, lane_groups, activate, 0)
        if far_in:
            pull[1].wait()
        top = (state.shape[0] - act_rows) // 2
        if blocks:
            for copy in copies:
                copy.wait()

        def multiply(n, carry):
            lanes = pl.ds(pl.multiple_of(n * wide, wide), wide)
            if not blocks:
                chunk_copy(n).wait()
            rows = w_s[:, :, lanes].reshape(width, wide)
            product = jnp.dot(act_s[...], rows, preferred_element_type=jnp.float32)
            old = state[top : top + act_rows, lanes].astype(jnp.float32)
            state_out[:, lanes] = (old + product).astype(jnp.bfloat16)
            return carry

        lax.fori_loop(0, chunks, multiply, 0)
        normed_from = state_out
        if far_out:
            push_state = pltpu.make_async_copy(state_out, state_hbm_out, out_sems.at[0])
            push_state.start()
    else:
        state_out[...] = state[...]
        normed_from = state

    if do_conv:
        block = 32

        def norm_rows(i, carry):
            row = pl.multiple_of(i * block, block)
            x = normed_from[pl.ds(row, block), :].astype(jnp.float32)
            mean = jnp.mean(x, axis=1, keepdims=True)
            x = x - mean
            var = jnp.mean(x * x, axis=1, keepdims=True)
            y = x * (lax.rsqrt(var + EPSILON) * row_valid(row, block, 1))
            y = y.astype(jnp.bfloat16).astype(jnp.float32)
            for g in range(lane_groups):
                norm_s[g, pl.ds(row, block), :] = y[:, g * LANES : (g + 1) * LANES]
            return carry

        lax.fori_loop(0, act_rows // block, norm_rows, 0)
        for copy in tap_copies:
            copy.wait()
        out_rows = act_rows - taps_n
        edge = (out_rows - own) // 2
        mask_s[...] = row_valid(edge + taps_n // 2, own, LANES)
        tiles = out_rows // SUBLANES
        splits, run = conv_split(out_rows)

        def conv_lanes(g, carry):
            lanes = pl.ds(pl.multiple_of(g * LANES, LANES), LANES)
            for b in range(splits):
                base = b * (tiles // splits) * SUBLANES
                tap = [
                    jnp.broadcast_to(taps[k : k + 1, lanes].astype(jnp.float32), (SUBLANES, LANES))
                    for k in range(taps_n)
                ]
                acc = [None] * run
                for m in range(run + taps_n - 1):
                    v = norm_s[g, pl.ds(base + m, SUBLANES, stride=run), :]
                    for j in range(run):
                        if 0 <= m - j < taps_n:
                            term = tap[m - j] * v
                            acc[j] = term if acc[j] is None else acc[j] + term
                for j in range(run):
                    mix_s[pl.ds(base + j, SUBLANES, stride=run), :] = acc[j]
            mixed_out[:, lanes] = mix_s[:out_rows, :].astype(jnp.bfloat16)
            if far_out:
                pltpu.make_async_copy(
                    mixed_out.at[:, lanes], mixed_hbm_out.at[:, lanes], out_sems.at[1]
                ).start()
            mine = mix_s[edge : edge + own, :]
            masked = mine * mask_s[...]
            one = jnp.sum(masked, axis=0, keepdims=True)
            two = jnp.sum(masked * mine, axis=0, keepdims=True)
            both = jnp.concatenate([one, two], axis=0)
            for c in range(sums_out.shape[0]):
                sums_out[c, :, lanes] = both
            return carry

        lax.fori_loop(0, lane_groups, conv_lanes, 0)
        if far_out:
            push_state.wait()
            pltpu.make_async_copy(mixed_out, mixed_hbm_out, out_sems.at[1]).wait()


def conv_split(out_rows):
    tiles = out_rows // SUBLANES
    splits = 1 if tiles <= 24 else 2
    run = tiles // splits
    return splits, run + (run % SUBLANES == 0)


def run_module(scal, state, z, own, layer, rim, copies, prev, do_conv, far):
    width = state.shape[1]
    chunks = 6
    taps_n = 2 * rim
    do_mm = prev is not None
    vmem = pl.BlockSpec(memory_space=pltpu.VMEM)
    hbm = pl.BlockSpec(memory_space=pltpu.HBM)
    args, specs = [scal], [pl.BlockSpec(memory_space=pltpu.SMEM)]
    scratch = []
    group_at, blocks = 0, ()
    act_rows = state.shape[0]
    if do_mm:
        mixed, sums, others, parts, group_at = prev
        act_rows = mixed.shape[0]
        args += [mixed, sums, others, *parts]
        specs += [hbm if far[0] else vmem] + [vmem] * 2 + [hbm] * len(parts)
        rows = parts[0].shape[2]
        if len(parts) > 1:
            blocks = tuple(p.shape[0] for p in parts)
        scratch += [
            pltpu.VMEM((act_rows, width), jnp.bfloat16),
            pltpu.VMEM((width // rows, rows, width), jnp.bfloat16),
            pltpu.SemaphoreType.DMA((max(chunks, sum(blocks)),)),
            pltpu.VMEM((2, EXTRA, width), jnp.bfloat16),
            pltpu.VMEM((2, width), jnp.float32),
        ]
    args += [state, *z]
    specs += [hbm if far[0] else vmem, hbm, hbm]
    shapes = [jax.ShapeDtypeStruct((act_rows, width), jnp.bfloat16)]
    if do_conv:
        out_rows = act_rows - taps_n
        splits, run = conv_split(out_rows)
        more = SUBLANES * (run - out_rows // SUBLANES // splits)
        scratch += [
            pltpu.VMEM((width // LANES, act_rows + more, LANES), jnp.float32),
            pltpu.VMEM((own, LANES), jnp.float32),
            pltpu.VMEM((out_rows + more, LANES), jnp.float32),
            pltpu.VMEM((taps_n, width), jnp.bfloat16),
        ]
        shapes += [
            jax.ShapeDtypeStruct((out_rows, width), jnp.bfloat16),
            jax.ShapeDtypeStruct((copies, 2, width), jnp.float32),
        ]
    out_specs = [vmem] * len(shapes)
    scratch.append(pltpu.SemaphoreType.DMA((4,)))
    if far[0]:
        scratch += [
            pltpu.VMEM(mixed.shape, mixed.dtype),
            pltpu.VMEM(state.shape, state.dtype),
            pltpu.SemaphoreType.DMA((2,)),
        ]
    if far[1]:
        out_specs[0] = out_specs[1] = hbm
        shapes = [pltpu.HBM(a.shape, a.dtype) for a in shapes[:2]] + shapes[2:]
        scratch += [
            pltpu.VMEM(shapes[1].shape, shapes[1].dtype),
            pltpu.VMEM(shapes[0].shape, shapes[0].dtype),
            pltpu.SemaphoreType.DMA((2,)),
        ]
    plan = (
        do_mm, do_conv, layer, act_rows, own, layer * rim, chunks, group_at, taps_n, blocks, far
    )
    args = [
        pltpu.with_memory_space_constraint(a, pltpu.HBM) if spec is hbm else a
        for a, spec in zip(args, specs)
    ]
    return pl.pallas_call(
        functools.partial(module_kernel, plan),
        out_shape=shapes,
        in_specs=specs,
        out_specs=out_specs,
        scratch_shapes=scratch,
        compiler_params=pltpu.CompilerParams(vmem_limit_bytes=32 << 20),
        name="module_step",
    )(*args)


SIDE = 4
STEPS = (0, 1, 3, 2)


def line_shift(steps, turned):
    pairs = []
    for p in range(SIDE):
        for q in range(SIDE):
            for core in range(2):
                to = (p, (q + steps) % SIDE) if core != turned else ((p + steps) % SIDE, q)
                pairs.append(((p * SIDE + q) * 2 + core, (to[0] * SIDE + to[1]) * 2 + core))
    return pairs


def along(x, steps):
    return lax.ppermute(x, ("ctx", "dp"), line_shift(steps, 0))


def across(x, steps):
    return lax.ppermute(x, ("ctx", "dp"), line_shift(steps, 1))


def plane_places():
    places = []
    for x in range(SIDE):
        for y in range(SIDE):
            by_core = [
                [((x - p) % SIDE * SIDE + (y - q) % SIDE) * 2 for q in STEPS for p in STEPS],
                [((x - q) % SIDE * SIDE + (y - p) % SIDE) * 2 + 1 for q in STEPS for p in STEPS],
            ]
            places += [by_core[0] + by_core[1], by_core[1] + by_core[0]]
    return jnp.array(places, jnp.int32)


STAGES = ((1, 4), (4, 8))


def shards(frames_in, lengths, depth_kernel, batch_gain, batch_bias, out_weight):
    layer_total = lax.axis_size("segment")
    ctx_count = lax.axis_size("ctx")
    segment_index = lax.axis_index("segment")
    ctx_index = lax.axis_index("ctx")
    dp_index = lax.axis_index("dp")
    frames_dev = frames_in.shape[2]
    kernel_size = depth_kernel.shape[1]
    rim = kernel_size // 2
    both = [(0, 1), (1, 0)]
    forward = [(i, i + 1) for i in range(ctx_count - 1)]
    backward = [(b, a) for a, b in forward]

    half_rows = out_weight.shape[1] // 2
    mine = lax.dynamic_slice_in_dim(out_weight[0], dp_index * half_rows, half_rows, 0)
    scales = jnp.where(dp_index == 0, batch_gain, batch_bias)
    upper = lax.reduce_precision(scales, 8, 7)
    scales = jnp.concatenate([upper, scales - upper], axis=0).astype(jnp.bfloat16)
    mine_taps = lax.dynamic_slice_in_dim(depth_kernel[0], dp_index * rim, rim, 0)
    pad = jnp.zeros((EXTRA - scales.shape[0], scales.shape[1]), jnp.bfloat16)
    mine = jnp.concatenate([mine, mine_taps.astype(jnp.bfloat16), scales, pad], axis=0)

    def shift(x, steps):
        pairs = [(i, (i + steps) % layer_total) for i in range(layer_total)]
        return lax.ppermute(x, "segment", pairs)

    def place(x, steps, row=0):
        at = (segment_index + steps) % layer_total
        return lax.dynamic_update_slice(ring, x[None], (at, row, 0))

    ring = jnp.broadcast_to(mine[None], (layer_total, *mine.shape))
    up = down = mine
    for steps in range(1, layer_total // 2):
        up, down = shift(up, 1), shift(down, -1)
        if steps == 1:
            lengths, up, down = lax.optimization_barrier((lengths, up, down))
        ring = place(up, -steps)
        ring = place(down, steps)
    ring = place(shift(up[:half_rows], 1), layer_total // 2)
    ring = place(shift(down[half_rows:], -1), layer_total // 2, half_rows)

    mine_len = lax.dynamic_slice_in_dim(lengths[0], segment_index, 1, 0)
    count = mine_len + lax.ppermute(mine_len, "dp", both)
    halo = rim * layer_total
    first = (ctx_index * frames_dev - halo).astype(jnp.int32)
    scal = [mine_len, first[None], count, dp_index[None]]
    at = ctx_index * 2 + dp_index
    places = lax.dynamic_index_in_dim(plane_places(), at, 0, keepdims=False)
    scal = jnp.concatenate([*scal, places])

    own = lax.dynamic_index_in_dim(frames_in[0], segment_index, 0, keepdims=False)
    low = lax.ppermute(own[frames_dev - halo :], "ctx", forward)
    high = lax.ppermute(own[:halo], "ctx", backward)
    state = jnp.concatenate([low, own, high], axis=0)

    ring, state, scal = lax.optimization_barrier((ring, state, scal))

    weights = {}

    def gather_stage(lo, hi, blocks):
        parts = [lax.all_gather(blocks[lo:hi, :half_rows], ("ctx", "dp"), axis=0)]
        for layer in range(lo, hi):
            weights[layer] = (parts, layer - lo)

    gather_stage(*STAGES[0], ring)
    line = ring[:1, :half_rows]
    line = [line] + [along(line, steps) for steps in STEPS[1:]]
    z = (ring, lax.ppermute(ring[:, half_rows:], "dp", both))
    waits = [lo for lo, _ in STAGES]

    prev = None
    for layer in range(layer_total):
        far = (layer - 1 in waits, layer in waits)
        state, mixed, sums = run_module(
            scal, state, z, frames_dev, layer, rim, ctx_count, prev, True, far
        )
        if layer == 0:
            line, late, sums = lax.optimization_barrier((line, ring, sums))
            for lo, hi in STAGES[1:]:
                gather_stage(lo, hi, late)
            line, sums = lax.optimization_barrier((jnp.stack(line), sums))
            parts = [line] + [across(line, steps) for steps in STEPS[1:]]
        sums = lax.all_to_all(sums, "ctx", 0, 0, tiled=True)
        if layer == 0:
            parts, sums = lax.optimization_barrier((parts, sums))
            weights[0] = (parts + [lax.ppermute(p, "dp", both) for p in parts], 0)
        others = lax.ppermute(sums, "dp", both)
        prev = (mixed, sums, others, *weights[layer])
    far = (False, False)
    (state,) = run_module(
        scal, state, z, frames_dev, layer_total, rim, ctx_count, prev, False, far
    )
    return state[None, None]


def solution(mesh):
    placed = (
        P("dp", None, "ctx", None),
        P("dp", None),
        P("segment", None, None),
        P("segment", None),
        P("segment", None),
        P("segment", "ctx", None),
    )
    return jax.shard_map(
        shards,
        mesh=mesh,
        in_specs=placed,
        out_specs=P("dp", "segment", "ctx", None),
        check_vma=False,
    )
```

```python
import functools

import jax
import jax.numpy as jnp
from jax import lax
from jax.experimental import pallas as pl
from jax.experimental.pallas import tpu as pltpu
from jax.sharding import PartitionSpec as P

EPSILON = 1e-05
LANES = 128
SUBLANES = 8
EXTRA = 8


def module_kernel(plan, *refs):
    do_mm, do_conv, layer, act_rows, own, first_at, chunks, group_at, taps_n, blocks, far = plan
    far_in, far_out = far
    refs = list(refs)
    scal = refs.pop(0)
    if do_mm:
        mixed, sums, others, gb = [refs.pop(0) for _ in range(4)]
        w_parts = [refs.pop(0) for _ in range(max(1, len(blocks)))]
    state, ring, other = [refs.pop(0) for _ in range(3)]
    state_out = refs.pop(0)
    if do_conv:
        mixed_out, sums_out, gb_next = [refs.pop(0) for _ in range(3)]
    if do_mm:
        act_s, w_s, sems, affine = [refs.pop(0) for _ in range(4)]
    if do_conv:
        norm_s, mask_s, mix_s, taps = [refs.pop(0) for _ in range(4)]
    z_sems = refs.pop(0)
    if far_in:
        mixed_hbm, state_hbm = mixed, state
        mixed, state, in_sems = [refs.pop(0) for _ in range(3)]
        pull = [
            pltpu.make_async_copy(mixed_hbm, mixed, in_sems.at[0]),
            pltpu.make_async_copy(state_hbm, state, in_sems.at[1]),
        ]
        for copy in pull:
            copy.start()
    if far_out:
        mixed_hbm_out, state_hbm_out = mixed_out, state_out
        mixed_out, state_out, out_sems = [refs.pop(0) for _ in range(3)]

    core = scal[3]
    half_taps = taps_n // 2
    rows_at = ring.shape[1] - half_taps - EXTRA

    if do_conv:
        at = layer
        to = [pl.ds(pl.multiple_of(c * half_taps, half_taps), half_taps) for c in (core, 1 - core)]
        tap_copies = [
            pltpu.make_async_copy(
                ring.at[at, pl.ds(rows_at, half_taps)], taps.at[to[0]], z_sems.at[2]
            ),
            pltpu.make_async_copy(
                other.at[at, pl.ds(0, half_taps)], taps.at[to[1]], z_sems.at[3]
            ),
        ]
        gb_copies = [
            pltpu.make_async_copy(
                ring.at[at, pl.ds(rows_at + half_taps, EXTRA)], gb_next.at[core], z_sems.at[0]
            ),
            pltpu.make_async_copy(
                other.at[at, pl.ds(half_taps, EXTRA)], gb_next.at[1 - core], z_sems.at[1]
            ),
        ]
        for copy in tap_copies + gb_copies:
            copy.start()

    width = state.shape[1]
    length = scal[0]
    first = scal[1] + first_at
    lane_groups = width // LANES

    def row_valid(row, rows, lanes):
        at = lax.broadcasted_iota(jnp.int32, (rows, lanes), 0) + (first + row)
        return jnp.where((at >= 0) & (at < length), 1.0, 0.0).astype(jnp.float32)

    if do_mm:
        wide = width // chunks
        copies = []
        if blocks:
            for part, count in zip(w_parts, blocks):
                for i in range(count):
                    n = len(copies)
                    copies.append(
                        pltpu.make_async_copy(
                            part.at[i, group_at], w_s.at[scal[4 + n]], sems.at[n]
                        )
                    )

        def chunk_copy(n):
            lanes = pl.ds(pl.multiple_of(n * wide, wide), wide)
            return pltpu.make_async_copy(
                w_parts[0].at[:, group_at, :, lanes], w_s.at[:, :, lanes], sems.at[n]
            )

        if not blocks:
            copies = [chunk_copy(n) for n in range(chunks)]
        for copy in copies:
            copy.start()
        total = sums[0] + others[0]
        for s in range(1, sums.shape[0]):
            total = total + sums[s] + others[s]
        count = scal[2].astype(jnp.float32)
        mean = total[0:1] / count
        var = total[1:2] / count - mean * mean
        gain, bias = gb[0].astype(jnp.float32), gb[1].astype(jnp.float32)
        scale = lax.rsqrt(var + EPSILON) * (gain[0:1] + gain[1:2])
        shift = (bias[0:1] + bias[1:2]) - mean * scale
        affine[0:1, :] = 0.5 * scale
        affine[1:2, :] = 0.5 * shift
        valid = row_valid(0, act_rows, LANES)

        def activate(g, carry):
            lanes = pl.ds(pl.multiple_of(g * LANES, LANES), LANES)
            half = mixed[:, lanes].astype(jnp.float32) * affine[0:1, lanes] + affine[1:2, lanes]
            act = (half + half * jnp.tanh(half)) * valid
            act_s[:, lanes] = act.astype(jnp.bfloat16)
            return carry

        if far_in:
            pull[0].wait()
        lax.fori_loop(0, lane_groups, activate, 0)
        if far_in:
            pull[1].wait()
        top = (state.shape[0] - act_rows) // 2
        if blocks:
            for copy in copies:
                copy.wait()

        def multiply(n, carry):
            lanes = pl.ds(pl.multiple_of(n * wide, wide), wide)
            if not blocks:
                chunk_copy(n).wait()
            rows = w_s[:, :, lanes].reshape(width, wide)
            product = jnp.dot(act_s[...], rows, preferred_element_type=jnp.float32)
            old = state[top : top + act_rows, lanes].astype(jnp.float32)
            state_out[:, lanes] = (old + product).astype(jnp.bfloat16)
            return carry

        lax.fori_loop(0, chunks, multiply, 0)
        normed_from = state_out
        if far_out:
            push_state = pltpu.make_async_copy(state_out, state_hbm_out, out_sems.at[0])
            push_state.start()
    else:
        state_out[...] = state[...]
        normed_from = state

    if do_conv:
        block = 32

        def norm_rows(i, carry):
            row = pl.multiple_of(i * block, block)
            x = normed_from[pl.ds(row, block), :].astype(jnp.float32)
            mean = jnp.mean(x, axis=1, keepdims=True)
            x = x - mean
            var = jnp.mean(x * x, axis=1, keepdims=True)
            y = x * (lax.rsqrt(var + EPSILON) * row_valid(row, block, 1))
            y = y.astype(jnp.bfloat16).astype(jnp.float32)
            for g in range(lane_groups):
                norm_s[g, pl.ds(row, block), :] = y[:, g * LANES : (g + 1) * LANES]
            return carry

        lax.fori_loop(0, act_rows // block, norm_rows, 0)
        for copy in tap_copies:
            copy.wait()
        out_rows = act_rows - taps_n
        edge = (out_rows - own) // 2
        mask_s[...] = row_valid(edge + taps_n // 2, own, LANES)
        tiles = out_rows // SUBLANES
        splits, run = conv_split(out_rows)

        def conv_lanes(g, carry):
            lanes = pl.ds(pl.multiple_of(g * LANES, LANES), LANES)
            for b in range(splits):
                base = b * (tiles // splits) * SUBLANES
                tap = [
                    jnp.broadcast_to(taps[k : k + 1, lanes].astype(jnp.float32), (SUBLANES, LANES))
                    for k in range(taps_n)
                ]
                acc = [None] * run
                for m in range(run + taps_n - 1):
                    v = norm_s[g, pl.ds(base + m, SUBLANES, stride=run), :]
                    for j in range(run):
                        if 0 <= m - j < taps_n:
                            term = tap[m - j] * v
                            acc[j] = term if acc[j] is None else acc[j] + term
                for j in range(run):
                    mix_s[pl.ds(base + j, SUBLANES, stride=run), :] = acc[j]
            mixed_out[:, lanes] = mix_s[:out_rows, :].astype(jnp.bfloat16)
            if far_out:
                pltpu.make_async_copy(
                    mixed_out.at[:, lanes], mixed_hbm_out.at[:, lanes], out_sems.at[1]
                ).start()
            mine = mix_s[edge : edge + own, :]
            masked = mine * mask_s[...]
            one = jnp.sum(masked, axis=0, keepdims=True)
            two = jnp.sum(masked * mine, axis=0, keepdims=True)
            both = jnp.concatenate([one, two], axis=0)
            for c in range(sums_out.shape[0]):
                sums_out[c, :, lanes] = both
            return carry

        lax.fori_loop(0, lane_groups, conv_lanes, 0)
        for copy in gb_copies:
            copy.wait()
        if far_out:
            push_state.wait()
            pltpu.make_async_copy(mixed_out, mixed_hbm_out, out_sems.at[1]).wait()


def conv_split(out_rows):
    tiles = out_rows // SUBLANES
    splits = 1 if tiles <= 24 else 2
    run = tiles // splits
    return splits, run + (run % SUBLANES == 0)


def run_module(scal, state, z, own, layer, rim, copies, prev, do_conv, far):
    width = state.shape[1]
    chunks = 6
    taps_n = 2 * rim
    do_mm = prev is not None
    vmem = pl.BlockSpec(memory_space=pltpu.VMEM)
    hbm = pl.BlockSpec(memory_space=pltpu.HBM)
    args, specs = [scal], [pl.BlockSpec(memory_space=pltpu.SMEM)]
    scratch = []
    group_at, blocks = 0, ()
    act_rows = state.shape[0]
    if do_mm:
        mixed, sums, others, gb, parts, group_at = prev
        act_rows = mixed.shape[0]
        args += [mixed, sums, others, gb, *parts]
        specs += [hbm if far[0] else vmem] + [vmem] * 3 + [hbm] * len(parts)
        rows = parts[0].shape[2]
        if len(parts) > 1:
            blocks = tuple(p.shape[0] for p in parts)
        scratch += [
            pltpu.VMEM((act_rows, width), jnp.bfloat16),
            pltpu.VMEM((width // rows, rows, width), jnp.bfloat16),
            pltpu.SemaphoreType.DMA((max(chunks, sum(blocks)),)),
            pltpu.VMEM((2, width), jnp.float32),
        ]
    args += [state, *z]
    specs += [hbm if far[0] else vmem, hbm, hbm]
    shapes = [jax.ShapeDtypeStruct((act_rows, width), jnp.bfloat16)]
    if do_conv:
        out_rows = act_rows - taps_n
        splits, run = conv_split(out_rows)
        more = SUBLANES * (run - out_rows // SUBLANES // splits)
        scratch += [
            pltpu.VMEM((width // LANES, act_rows + more, LANES), jnp.float32),
            pltpu.VMEM((own, LANES), jnp.float32),
            pltpu.VMEM((out_rows + more, LANES), jnp.float32),
            pltpu.VMEM((taps_n, width), jnp.bfloat16),
        ]
        shapes += [
            jax.ShapeDtypeStruct((out_rows, width), jnp.bfloat16),
            jax.ShapeDtypeStruct((copies, 2, width), jnp.float32),
            jax.ShapeDtypeStruct((2, EXTRA, width), jnp.bfloat16),
        ]
    out_specs = [vmem] * len(shapes)
    scratch.append(pltpu.SemaphoreType.DMA((4,)))
    if far[0]:
        scratch += [
            pltpu.VMEM(mixed.shape, mixed.dtype),
            pltpu.VMEM(state.shape, state.dtype),
            pltpu.SemaphoreType.DMA((2,)),
        ]
    if far[1]:
        out_specs[0] = out_specs[1] = hbm
        shapes = [pltpu.HBM(a.shape, a.dtype) for a in shapes[:2]] + shapes[2:]
        scratch += [
            pltpu.VMEM(shapes[1].shape, shapes[1].dtype),
            pltpu.VMEM(shapes[0].shape, shapes[0].dtype),
            pltpu.SemaphoreType.DMA((2,)),
        ]
    plan = (
        do_mm, do_conv, layer, act_rows, own, layer * rim, chunks, group_at, taps_n, blocks, far
    )
    args = [
        pltpu.with_memory_space_constraint(a, pltpu.HBM) if spec is hbm else a
        for a, spec in zip(args, specs)
    ]
    return pl.pallas_call(
        functools.partial(module_kernel, plan),
        out_shape=shapes,
        in_specs=specs,
        out_specs=out_specs,
        scratch_shapes=scratch,
        compiler_params=pltpu.CompilerParams(vmem_limit_bytes=32 << 20),
        name="module_step",
    )(*args)


SIDE = 4
STEPS = (0, 1, 3, 2)


def line_shift(steps, turned):
    pairs = []
    for p in range(SIDE):
        for q in range(SIDE):
            for core in range(2):
                to = (p, (q + steps) % SIDE) if core != turned else ((p + steps) % SIDE, q)
                pairs.append(((p * SIDE + q) * 2 + core, (to[0] * SIDE + to[1]) * 2 + core))
    return pairs


def along(x, steps):
    return lax.ppermute(x, ("ctx", "dp"), line_shift(steps, 0))


def across(x, steps):
    return lax.ppermute(x, ("ctx", "dp"), line_shift(steps, 1))


def plane_places():
    places = []
    for x in range(SIDE):
        for y in range(SIDE):
            by_core = [
                [((x - p) % SIDE * SIDE + (y - q) % SIDE) * 2 for q in STEPS for p in STEPS],
                [((x - q) % SIDE * SIDE + (y - p) % SIDE) * 2 + 1 for q in STEPS for p in STEPS],
            ]
            places += [by_core[0] + by_core[1], by_core[1] + by_core[0]]
    return jnp.array(places, jnp.int32)


STAGES = ((1, 5), (5, 8))


def shards(frames_in, lengths, depth_kernel, batch_gain, batch_bias, out_weight):
    layer_total = lax.axis_size("segment")
    ctx_count = lax.axis_size("ctx")
    segment_index = lax.axis_index("segment")
    ctx_index = lax.axis_index("ctx")
    dp_index = lax.axis_index("dp")
    frames_dev = frames_in.shape[2]
    kernel_size = depth_kernel.shape[1]
    rim = kernel_size // 2
    both = [(0, 1), (1, 0)]
    forward = [(i, i + 1) for i in range(ctx_count - 1)]
    backward = [(b, a) for a, b in forward]

    half_rows = out_weight.shape[1] // 2
    mine = lax.dynamic_slice_in_dim(out_weight[0], dp_index * half_rows, half_rows, 0)
    scales = jnp.where(dp_index == 0, batch_gain, batch_bias)
    upper = lax.reduce_precision(scales, 8, 7)
    scales = jnp.concatenate([upper, scales - upper], axis=0).astype(jnp.bfloat16)
    mine_taps = lax.dynamic_slice_in_dim(depth_kernel[0], dp_index * rim, rim, 0)
    pad = jnp.zeros((EXTRA - scales.shape[0], scales.shape[1]), jnp.bfloat16)
    mine = jnp.concatenate([mine, mine_taps.astype(jnp.bfloat16), scales, pad], axis=0)

    def shift(x, steps):
        pairs = [(i, (i + steps) % layer_total) for i in range(layer_total)]
        return lax.ppermute(x, "segment", pairs)

    def place(x, steps, row=0):
        at = (segment_index + steps) % layer_total
        return lax.dynamic_update_slice(ring, x[None], (at, row, 0))

    ring = jnp.broadcast_to(mine[None], (layer_total, *mine.shape))
    up = down = mine
    for steps in range(1, layer_total // 2):
        up, down = shift(up, 1), shift(down, -1)
        if steps == 1:
            lengths, up, down = lax.optimization_barrier((lengths, up, down))
        ring = place(up, -steps)
        ring = place(down, steps)
    ring = place(shift(up[:half_rows], 1), layer_total // 2)
    ring = place(shift(down[half_rows:], -1), layer_total // 2, half_rows)

    mine_len = lax.dynamic_slice_in_dim(lengths[0], segment_index, 1, 0)
    count = mine_len + lax.ppermute(mine_len, "dp", both)
    halo = rim * layer_total
    first = (ctx_index * frames_dev - halo).astype(jnp.int32)
    scal = [mine_len, first[None], count, dp_index[None]]
    at = ctx_index * 2 + dp_index
    places = lax.dynamic_index_in_dim(plane_places(), at, 0, keepdims=False)
    scal = jnp.concatenate([*scal, places])

    own = lax.dynamic_index_in_dim(frames_in[0], segment_index, 0, keepdims=False)
    low = lax.ppermute(own[frames_dev - halo :], "ctx", forward)
    high = lax.ppermute(own[:halo], "ctx", backward)
    low, high, _ = lax.optimization_barrier((low, high, up))
    state = jnp.concatenate([low, own, high], axis=0)

    ring, state, scal = lax.optimization_barrier((ring, state, scal))

    weights = {}

    def gather_stage(lo, hi, blocks):
        parts = [lax.all_gather(blocks[lo:hi, :half_rows], ("ctx", "dp"), axis=0)]
        for layer in range(lo, hi):
            weights[layer] = (parts, layer - lo)

    gather_stage(*STAGES[0], ring)
    line = ring[:1, :half_rows]
    line = [line] + [along(line, steps) for steps in STEPS[1:]]
    z = (ring, lax.ppermute(ring[:, half_rows:], "dp", both))
    waits = [lo for lo, _ in STAGES]

    prev = None
    for layer in range(layer_total):
        far = (layer - 1 in waits, layer in waits)
        state, mixed, sums, gb = run_module(
            scal, state, z, frames_dev, layer, rim, ctx_count, prev, True, far
        )
        if layer == 0:
            line, late, sums = lax.optimization_barrier((line, ring, sums))
            for lo, hi in STAGES[1:]:
                gather_stage(lo, hi, late)
            line, sums = lax.optimization_barrier((jnp.stack(line), sums))
            parts = [line] + [across(line, steps) for steps in STEPS[1:]]
        sums = lax.all_to_all(sums, "ctx", 0, 0, tiled=True)
        if layer == 0:
            parts, sums = lax.optimization_barrier((parts, sums))
            weights[0] = (parts + [lax.ppermute(p, "dp", both) for p in parts], 0)
        others = lax.ppermute(sums, "dp", both)
        prev = (mixed, sums, others, gb, *weights[layer])
    far = (False, False)
    (state,) = run_module(
        scal, state, z, frames_dev, layer_total, rim, ctx_count, prev, False, far
    )
    return state[None, None]


def solution(mesh):
    placed = (
        P("dp", None, "ctx", None),
        P("dp", None),
        P("segment", None, None),
        P("segment", None),
        P("segment", None),
        P("segment", "ctx", None),
    )
    return jax.shard_map(
        shards,
        mesh=mesh,
        in_specs=placed,
        out_specs=P("dp", "segment", "ctx", None),
        check_vma=False,
    )
```

```python
import functools

import jax
import jax.numpy as jnp
from jax import lax
from jax.experimental import pallas as pl
from jax.experimental.pallas import tpu as pltpu
from jax.sharding import PartitionSpec as P

EPSILON = 1e-05
LANES = 128
SUBLANES = 8
EXTRA = 8


def module_kernel(plan, *refs):
    do_mm, do_conv, layer, act_rows, own, first_at, chunks, group_at, taps_n, blocks, far, fetch = plan
    far_in, far_out = far
    held, next_at = fetch
    refs = list(refs)
    scal = refs.pop(0)
    if do_mm:
        mixed, sums, others, gb = [refs.pop(0) for _ in range(4)]
        w_parts = [refs.pop(0) for _ in range(max(1, len(blocks)))]
    state, ring, other = [refs.pop(0) for _ in range(3)]
    next_hbm = refs.pop(0) if next_at is not None else None
    state_out = refs.pop(0)
    if do_conv:
        mixed_out, sums_out, gb_next = [refs.pop(0) for _ in range(3)]
    w_next = refs.pop(0) if next_at is not None else None
    if do_mm:
        act_s, affine = refs.pop(0), refs.pop(0)
        w_s, sems = (w_parts[0], None) if held else (refs.pop(0), refs.pop(0))
    if do_conv:
        norm_s, mask_s, mix_s, taps = [refs.pop(0) for _ in range(4)]
    z_sems = refs.pop(0)
    if next_at is not None:
        next_copy = pltpu.make_async_copy(next_hbm.at[:, next_at], w_next, z_sems.at[4])
        if held:
            next_copy.start()
    if far_in:
        mixed_hbm, state_hbm = mixed, state
        mixed, state, in_sems = [refs.pop(0) for _ in range(3)]
        pull = [
            pltpu.make_async_copy(mixed_hbm, mixed, in_sems.at[0]),
            pltpu.make_async_copy(state_hbm, state, in_sems.at[1]),
        ]
        for copy in pull:
            copy.start()
    if far_out:
        mixed_hbm_out, state_hbm_out = mixed_out, state_out
        mixed_out, state_out, out_sems = [refs.pop(0) for _ in range(3)]

    core = scal[3]
    half_taps = taps_n // 2
    rows_at = ring.shape[1] - half_taps - EXTRA

    if do_conv:
        at = layer
        to = [pl.ds(pl.multiple_of(c * half_taps, half_taps), half_taps) for c in (core, 1 - core)]
        tap_copies = [
            pltpu.make_async_copy(
                ring.at[at, pl.ds(rows_at, half_taps)], taps.at[to[0]], z_sems.at[2]
            ),
            pltpu.make_async_copy(
                other.at[at, pl.ds(0, half_taps)], taps.at[to[1]], z_sems.at[3]
            ),
        ]
        gb_copies = [
            pltpu.make_async_copy(
                ring.at[at, pl.ds(rows_at + half_taps, EXTRA)], gb_next.at[core], z_sems.at[0]
            ),
            pltpu.make_async_copy(
                other.at[at, pl.ds(half_taps, EXTRA)], gb_next.at[1 - core], z_sems.at[1]
            ),
        ]
        for copy in tap_copies + gb_copies:
            copy.start()

    width = state.shape[1]
    length = scal[0]
    first = scal[1] + first_at
    lane_groups = width // LANES

    def row_valid(row, rows, lanes):
        at = lax.broadcasted_iota(jnp.int32, (rows, lanes), 0) + (first + row)
        return jnp.where((at >= 0) & (at < length), 1.0, 0.0).astype(jnp.float32)

    if do_mm:
        wide = width // chunks
        copies = []
        if blocks:
            for part, count in zip(w_parts, blocks):
                for i in range(count):
                    n = len(copies)
                    copies.append(
                        pltpu.make_async_copy(
                            part.at[i, group_at], w_s.at[scal[4 + n]], sems.at[n]
                        )
                    )

        def chunk_copy(n):
            lanes = pl.ds(pl.multiple_of(n * wide, wide), wide)
            return pltpu.make_async_copy(
                w_parts[0].at[:, group_at, :, lanes], w_s.at[:, :, lanes], sems.at[n]
            )

        if not blocks and not held:
            copies = [chunk_copy(n) for n in range(chunks)]
        for copy in copies:
            copy.start()
        total = sums[0] + others[0]
        for s in range(1, sums.shape[0]):
            total = total + sums[s] + others[s]
        count = scal[2].astype(jnp.float32)
        mean = total[0:1] / count
        var = total[1:2] / count - mean * mean
        gain, bias = gb[0].astype(jnp.float32), gb[1].astype(jnp.float32)
        scale = lax.rsqrt(var + EPSILON) * (gain[0:1] + gain[1:2])
        shift = (bias[0:1] + bias[1:2]) - mean * scale
        affine[0:1, :] = 0.5 * scale
        affine[1:2, :] = 0.5 * shift
        valid = row_valid(0, act_rows, LANES)

        def activate(g, carry):
            lanes = pl.ds(pl.multiple_of(g * LANES, LANES), LANES)
            half = mixed[:, lanes].astype(jnp.float32) * affine[0:1, lanes] + affine[1:2, lanes]
            act = (half + half * jnp.tanh(half)) * valid
            act_s[:, lanes] = act.astype(jnp.bfloat16)
            return carry

        if far_in:
            pull[0].wait()
        lax.fori_loop(0, lane_groups, activate, 0)
        if far_in:
            pull[1].wait()
        top = (state.shape[0] - act_rows) // 2
        if blocks:
            for copy in copies:
                copy.wait()

        def multiply(n, carry):
            lanes = pl.ds(pl.multiple_of(n * wide, wide), wide)
            if not blocks and not held:
                chunk_copy(n).wait()
            rows = w_s[:, :, lanes].reshape(width, wide)
            product = jnp.dot(act_s[...], rows, preferred_element_type=jnp.float32)
            old = state[top : top + act_rows, lanes].astype(jnp.float32)
            state_out[:, lanes] = (old + product).astype(jnp.bfloat16)
            return carry

        lax.fori_loop(0, chunks, multiply, 0)
        if next_at is not None and not held:
            next_copy.start()
        normed_from = state_out
        if far_out:
            push_state = pltpu.make_async_copy(state_out, state_hbm_out, out_sems.at[0])
            push_state.start()
    else:
        state_out[...] = state[...]
        normed_from = state

    if do_conv:
        block = 32

        def norm_rows(i, carry):
            row = pl.multiple_of(i * block, block)
            x = normed_from[pl.ds(row, block), :].astype(jnp.float32)
            mean = jnp.mean(x, axis=1, keepdims=True)
            x = x - mean
            var = jnp.mean(x * x, axis=1, keepdims=True)
            y = x * (lax.rsqrt(var + EPSILON) * row_valid(row, block, 1))
            y = y.astype(jnp.bfloat16).astype(jnp.float32)
            for g in range(lane_groups):
                norm_s[g, pl.ds(row, block), :] = y[:, g * LANES : (g + 1) * LANES]
            return carry

        lax.fori_loop(0, act_rows // block, norm_rows, 0)
        for copy in tap_copies:
            copy.wait()
        out_rows = act_rows - taps_n
        edge = (out_rows - own) // 2
        mask_s[...] = row_valid(edge + taps_n // 2, own, LANES)
        tiles = out_rows // SUBLANES
        splits, run = conv_split(out_rows)

        def conv_lanes(g, carry):
            lanes = pl.ds(pl.multiple_of(g * LANES, LANES), LANES)
            for b in range(splits):
                base = b * (tiles // splits) * SUBLANES
                tap = [
                    jnp.broadcast_to(taps[k : k + 1, lanes].astype(jnp.float32), (SUBLANES, LANES))
                    for k in range(taps_n)
                ]
                acc = [None] * run
                for m in range(run + taps_n - 1):
                    v = norm_s[g, pl.ds(base + m, SUBLANES, stride=run), :]
                    for j in range(run):
                        if 0 <= m - j < taps_n:
                            term = tap[m - j] * v
                            acc[j] = term if acc[j] is None else acc[j] + term
                for j in range(run):
                    mix_s[pl.ds(base + j, SUBLANES, stride=run), :] = acc[j]
            mixed_out[:, lanes] = mix_s[:out_rows, :].astype(jnp.bfloat16)
            if far_out:
                pltpu.make_async_copy(
                    mixed_out.at[:, lanes], mixed_hbm_out.at[:, lanes], out_sems.at[1]
                ).start()
            mine = mix_s[edge : edge + own, :]
            masked = mine * mask_s[...]
            one = jnp.sum(masked, axis=0, keepdims=True)
            two = jnp.sum(masked * mine, axis=0, keepdims=True)
            both = jnp.concatenate([one, two], axis=0)
            for c in range(sums_out.shape[0]):
                sums_out[c, :, lanes] = both
            return carry

        lax.fori_loop(0, lane_groups, conv_lanes, 0)
        for copy in gb_copies + ([next_copy] if next_at is not None else []):
            copy.wait()
        if far_out:
            push_state.wait()
            pltpu.make_async_copy(mixed_out, mixed_hbm_out, out_sems.at[1]).wait()


def conv_split(out_rows):
    tiles = out_rows // SUBLANES
    splits = 1 if tiles <= 24 else 2
    run = tiles // splits
    return splits, run + (run % SUBLANES == 0)


def run_module(scal, state, z, own, layer, rim, copies, prev, do_conv, far, coming=None):
    width = state.shape[1]
    chunks = 6
    taps_n = 2 * rim
    do_mm = prev is not None
    vmem = pl.BlockSpec(memory_space=pltpu.VMEM)
    hbm = pl.BlockSpec(memory_space=pltpu.HBM)
    args, specs = [scal], [pl.BlockSpec(memory_space=pltpu.SMEM)]
    scratch = []
    group_at, blocks, held = 0, (), False
    act_rows = state.shape[0]
    if do_mm:
        mixed, sums, others, gb, parts, group_at = prev
        act_rows = mixed.shape[0]
        args += [mixed, sums, others, gb, *parts]
        held = group_at is None
        specs += [hbm if far[0] else vmem] + [vmem] * 3 + [vmem if held else hbm] * len(parts)
        rows = parts[0].shape[-2]
        if len(parts) > 1:
            blocks = tuple(p.shape[0] for p in parts)
        scratch += [
            pltpu.VMEM((act_rows, width), jnp.bfloat16),
            pltpu.VMEM((2, width), jnp.float32),
        ]
        if not held:
            scratch += [
                pltpu.VMEM((width // rows, rows, width), jnp.bfloat16),
                pltpu.SemaphoreType.DMA((max(chunks, sum(blocks)),)),
            ]
    args += [state, *z]
    specs += [hbm if far[0] else vmem, hbm, hbm]
    if coming is not None:
        args.append(coming[0])
        specs.append(hbm)
    shapes = [jax.ShapeDtypeStruct((act_rows, width), jnp.bfloat16)]
    if do_conv:
        out_rows = act_rows - taps_n
        splits, run = conv_split(out_rows)
        more = SUBLANES * (run - out_rows // SUBLANES // splits)
        scratch += [
            pltpu.VMEM((width // LANES, act_rows + more, LANES), jnp.float32),
            pltpu.VMEM((own, LANES), jnp.float32),
            pltpu.VMEM((out_rows + more, LANES), jnp.float32),
            pltpu.VMEM((taps_n, width), jnp.bfloat16),
        ]
        shapes += [
            jax.ShapeDtypeStruct((out_rows, width), jnp.bfloat16),
            jax.ShapeDtypeStruct((copies, 2, width), jnp.float32),
            jax.ShapeDtypeStruct((2, EXTRA, width), jnp.bfloat16),
        ]
    if coming is not None:
        blocks_n, _, rows, _ = coming[0].shape
        shapes.append(jax.ShapeDtypeStruct((blocks_n, rows, width), jnp.bfloat16))
    out_specs = [vmem] * len(shapes)
    scratch.append(pltpu.SemaphoreType.DMA((5,)))
    if far[0]:
        scratch += [
            pltpu.VMEM(mixed.shape, mixed.dtype),
            pltpu.VMEM(state.shape, state.dtype),
            pltpu.SemaphoreType.DMA((2,)),
        ]
    if far[1]:
        out_specs[0] = out_specs[1] = hbm
        shapes = [pltpu.HBM(a.shape, a.dtype) for a in shapes[:2]] + shapes[2:]
        scratch += [
            pltpu.VMEM(shapes[1].shape, shapes[1].dtype),
            pltpu.VMEM(shapes[0].shape, shapes[0].dtype),
            pltpu.SemaphoreType.DMA((2,)),
        ]
    plan = (
        do_mm, do_conv, layer, act_rows, own, layer * rim, chunks, group_at, taps_n, blocks, far,
        (held, None if coming is None else coming[1]),
    )
    args = [
        pltpu.with_memory_space_constraint(a, pltpu.HBM) if spec is hbm else a
        for a, spec in zip(args, specs)
    ]
    return pl.pallas_call(
        functools.partial(module_kernel, plan),
        out_shape=shapes,
        in_specs=specs,
        out_specs=out_specs,
        scratch_shapes=scratch,
        compiler_params=pltpu.CompilerParams(vmem_limit_bytes=32 << 20),
        name="module_step",
    )(*args)


SIDE = 4
STEPS = (0, 1, 3, 2)


def line_shift(steps, turned):
    pairs = []
    for p in range(SIDE):
        for q in range(SIDE):
            for core in range(2):
                to = (p, (q + steps) % SIDE) if core != turned else ((p + steps) % SIDE, q)
                pairs.append(((p * SIDE + q) * 2 + core, (to[0] * SIDE + to[1]) * 2 + core))
    return pairs


def along(x, steps):
    return lax.ppermute(x, ("ctx", "dp"), line_shift(steps, 0))


def across(x, steps):
    return lax.ppermute(x, ("ctx", "dp"), line_shift(steps, 1))


def plane_places():
    places = []
    for x in range(SIDE):
        for y in range(SIDE):
            by_core = [
                [((x - p) % SIDE * SIDE + (y - q) % SIDE) * 2 for q in STEPS for p in STEPS],
                [((x - q) % SIDE * SIDE + (y - p) % SIDE) * 2 + 1 for q in STEPS for p in STEPS],
            ]
            places += [by_core[0] + by_core[1], by_core[1] + by_core[0]]
    return jnp.array(places, jnp.int32)


STAGES = ((1, 5), (5, 8))


def shards(frames_in, lengths, depth_kernel, batch_gain, batch_bias, out_weight):
    layer_total = lax.axis_size("segment")
    ctx_count = lax.axis_size("ctx")
    segment_index = lax.axis_index("segment")
    ctx_index = lax.axis_index("ctx")
    dp_index = lax.axis_index("dp")
    frames_dev = frames_in.shape[2]
    kernel_size = depth_kernel.shape[1]
    rim = kernel_size // 2
    both = [(0, 1), (1, 0)]
    forward = [(i, i + 1) for i in range(ctx_count - 1)]
    backward = [(b, a) for a, b in forward]

    half_rows = out_weight.shape[1] // 2
    mine = lax.dynamic_slice_in_dim(out_weight[0], dp_index * half_rows, half_rows, 0)
    scales = jnp.where(dp_index == 0, batch_gain, batch_bias)
    upper = lax.reduce_precision(scales, 8, 7)
    scales = jnp.concatenate([upper, scales - upper], axis=0).astype(jnp.bfloat16)
    mine_taps = lax.dynamic_slice_in_dim(depth_kernel[0], dp_index * rim, rim, 0)
    pad = jnp.zeros((EXTRA - scales.shape[0], scales.shape[1]), jnp.bfloat16)
    mine = jnp.concatenate([mine, mine_taps.astype(jnp.bfloat16), scales, pad], axis=0)

    def shift(x, steps):
        pairs = [(i, (i + steps) % layer_total) for i in range(layer_total)]
        return lax.ppermute(x, "segment", pairs)

    def place(x, steps, row=0):
        at = (segment_index + steps) % layer_total
        return lax.dynamic_update_slice(ring, x[None], (at, row, 0))

    ring = jnp.broadcast_to(mine[None], (layer_total, *mine.shape))
    up = down = mine
    for steps in range(1, layer_total // 2):
        up, down = shift(up, 1), shift(down, -1)
        if steps == 1:
            lengths, up, down = lax.optimization_barrier((lengths, up, down))
        ring = place(up, -steps)
        ring = place(down, steps)
    ring = place(shift(up[:half_rows], 1), layer_total // 2)
    ring = place(shift(down[half_rows:], -1), layer_total // 2, half_rows)

    mine_len = lax.dynamic_slice_in_dim(lengths[0], segment_index, 1, 0)
    count = mine_len + lax.ppermute(mine_len, "dp", both)
    halo = rim * layer_total
    first = (ctx_index * frames_dev - halo).astype(jnp.int32)
    scal = [mine_len, first[None], count, dp_index[None]]
    at = ctx_index * 2 + dp_index
    places = lax.dynamic_index_in_dim(plane_places(), at, 0, keepdims=False)
    scal = jnp.concatenate([*scal, places])

    own = lax.dynamic_index_in_dim(frames_in[0], segment_index, 0, keepdims=False)
    low = lax.ppermute(own[frames_dev - halo :], "ctx", forward)
    high = lax.ppermute(own[:halo], "ctx", backward)
    low, high, _ = lax.optimization_barrier((low, high, up))
    state = jnp.concatenate([low, own, high], axis=0)

    ring, state, scal = lax.optimization_barrier((ring, state, scal))

    weights = {}

    def gather_stage(lo, hi, blocks):
        parts = [lax.all_gather(blocks[lo:hi, :half_rows], ("ctx", "dp"), axis=0)]
        for layer in range(lo, hi):
            weights[layer] = (parts, layer - lo)

    gather_stage(*STAGES[0], ring)
    line = ring[:1, :half_rows]
    line = [line] + [along(line, steps) for steps in STEPS[1:]]
    z = (ring, lax.ppermute(ring[:, half_rows:], "dp", both))
    waits = [lo for lo, _ in STAGES]

    prev = None
    for layer in range(layer_total):
        far = (layer - 1 in waits, layer in waits)
        coming = None
        if layer > 1 and layer not in waits:
            parts, group_at = weights[layer]
            coming = (parts[0], group_at)
        state, mixed, sums, gb, *fetched = run_module(
            scal, state, z, frames_dev, layer, rim, ctx_count, prev, True, far, coming
        )
        if layer == 0:
            line, late, sums = lax.optimization_barrier((line, ring, sums))
            for lo, hi in STAGES[1:]:
                gather_stage(lo, hi, late)
            line, sums = lax.optimization_barrier((jnp.stack(line), sums))
            parts = [line] + [across(line, steps) for steps in STEPS[1:]]
        sums = lax.all_to_all(sums, "ctx", 0, 0, tiled=True)
        if layer == 0:
            parts, sums = lax.optimization_barrier((parts, sums))
            weights[0] = (parts + [lax.ppermute(p, "dp", both) for p in parts], 0)
        others = lax.ppermute(sums, "dp", both)
        prev = (mixed, sums, others, gb, *((fetched, None) if fetched else weights[layer]))
    far = (False, False)
    (state,) = run_module(
        scal, state, z, frames_dev, layer_total, rim, ctx_count, prev, False, far
    )
    return state[None, None]


def solution(mesh):
    placed = (
        P("dp", None, "ctx", None),
        P("dp", None),
        P("segment", None, None),
        P("segment", None),
        P("segment", None),
        P("segment", "ctx", None),
    )
    return jax.shard_map(
        shards,
        mesh=mesh,
        in_specs=placed,
        out_specs=P("dp", "segment", "ctx", None),
        check_vma=False,
    )
```

```python
import functools

import jax
import jax.numpy as jnp
from jax import lax
from jax.experimental import pallas as pl
from jax.experimental.pallas import tpu as pltpu
from jax.sharding import PartitionSpec as P

EPSILON = 1e-05
LANES = 128
SUBLANES = 8
EXTRA = 8


def module_kernel(plan, *refs):
    do_mm, do_conv, layer, act_rows, own, first_at, chunks, group_at, taps_n, blocks, far, fetch = plan
    far_in, far_out = far
    held, next_at = fetch
    refs = list(refs)
    scal = refs.pop(0)
    if do_mm:
        mixed, sums, others, gb = [refs.pop(0) for _ in range(4)]
        w_parts = [refs.pop(0) for _ in range(max(1, len(blocks)))]
    state, ring, other = [refs.pop(0) for _ in range(3)]
    next_hbm = refs.pop(0) if next_at is not None else None
    state_out = refs.pop(0)
    if do_conv:
        mixed_out, sums_out, gb_next = [refs.pop(0) for _ in range(3)]
    w_next = refs.pop(0) if next_at is not None else None
    if do_mm:
        act_s, affine = refs.pop(0), refs.pop(0)
        w_s, sems = (w_parts[0], None) if held else (refs.pop(0), refs.pop(0))
    if do_conv:
        norm_s, mask_s, mix_s, taps = [refs.pop(0) for _ in range(4)]
    z_sems = refs.pop(0)
    if next_at is not None:
        next_copy = pltpu.make_async_copy(next_hbm.at[:, next_at], w_next, z_sems.at[4])
        if held:
            next_copy.start()
    if far_in:
        mixed_hbm, state_hbm = mixed, state
        mixed, state, in_sems = [refs.pop(0) for _ in range(3)]
        pull = [
            pltpu.make_async_copy(mixed_hbm, mixed, in_sems.at[0]),
            pltpu.make_async_copy(state_hbm, state, in_sems.at[1]),
        ]
        for copy in pull:
            copy.start()
    if far_out:
        mixed_hbm_out, state_hbm_out = mixed_out, state_out
        mixed_out, state_out, out_sems = [refs.pop(0) for _ in range(3)]

    core = scal[3]
    half_taps = taps_n // 2
    rows_at = ring.shape[1] - half_taps - EXTRA

    if do_conv:
        at = layer
        to = [pl.ds(pl.multiple_of(c * half_taps, half_taps), half_taps) for c in (core, 1 - core)]
        tap_copies = [
            pltpu.make_async_copy(
                ring.at[at, pl.ds(rows_at, half_taps)], taps.at[to[0]], z_sems.at[2]
            ),
            pltpu.make_async_copy(
                other.at[at, pl.ds(0, half_taps)], taps.at[to[1]], z_sems.at[3]
            ),
        ]
        gb_copies = [
            pltpu.make_async_copy(
                ring.at[at, pl.ds(rows_at + half_taps, EXTRA)], gb_next.at[core], z_sems.at[0]
            ),
            pltpu.make_async_copy(
                other.at[at, pl.ds(half_taps, EXTRA)], gb_next.at[1 - core], z_sems.at[1]
            ),
        ]
        for copy in tap_copies + gb_copies:
            copy.start()

    width = state.shape[1]
    length = scal[0]
    first = scal[1] + first_at
    lane_groups = width // LANES

    def row_valid(row, rows, lanes):
        at = lax.broadcasted_iota(jnp.int32, (rows, lanes), 0) + (first + row)
        return jnp.where((at >= 0) & (at < length), 1.0, 0.0).astype(jnp.float32)

    if do_mm:
        wide = width // chunks
        copies = []
        if blocks:
            for part, count in zip(w_parts, blocks):
                for i in range(count):
                    n = len(copies)
                    copies.append(
                        pltpu.make_async_copy(
                            part.at[i, group_at], w_s.at[scal[4 + n]], sems.at[n]
                        )
                    )

        def chunk_copy(n):
            lanes = pl.ds(pl.multiple_of(n * wide, wide), wide)
            return pltpu.make_async_copy(
                w_parts[0].at[:, group_at, :, lanes], w_s.at[:, :, lanes], sems.at[n]
            )

        if not blocks and not held:
            copies = [chunk_copy(n) for n in range(chunks)]
        for copy in copies:
            copy.start()
        total = sums[0] + others[0]
        for s in range(1, sums.shape[0]):
            total = total + sums[s] + others[s]
        count = scal[2].astype(jnp.float32)
        mean = total[0:1] / count
        var = total[1:2] / count - mean * mean
        gain, bias = gb[0].astype(jnp.float32), gb[1].astype(jnp.float32)
        scale = lax.rsqrt(var + EPSILON) * (gain[0:1] + gain[1:2])
        shift = (bias[0:1] + bias[1:2]) - mean * scale
        affine[0:1, :] = 0.5 * scale
        affine[1:2, :] = 0.5 * shift
        valid = row_valid(0, act_rows, LANES)

        def activate(g, carry):
            lanes = pl.ds(pl.multiple_of(g * LANES, LANES), LANES)
            half = mixed[:, lanes].astype(jnp.float32) * affine[0:1, lanes] + affine[1:2, lanes]
            act = (half + half * jnp.tanh(half)) * valid
            act_s[:, lanes] = act.astype(jnp.bfloat16)
            return carry

        if far_in:
            pull[0].wait()
        lax.fori_loop(0, lane_groups, activate, 0)
        if far_in:
            pull[1].wait()
        top = (state.shape[0] - act_rows) // 2
        if blocks:
            for copy in copies:
                copy.wait()

        def multiply(n, carry):
            lanes = pl.ds(pl.multiple_of(n * wide, wide), wide)
            if not blocks and not held:
                chunk_copy(n).wait()
            rows = w_s[:, :, lanes].reshape(width, wide)
            product = jnp.dot(act_s[...], rows, preferred_element_type=jnp.float32)
            old = state[top : top + act_rows, lanes].astype(jnp.float32)
            state_out[:, lanes] = (old + product).astype(jnp.bfloat16)
            return carry

        lax.fori_loop(0, chunks, multiply, 0)
        if next_at is not None and not held:
            next_copy.start()
        normed_from = state_out
        if far_out:
            push_state = pltpu.make_async_copy(state_out, state_hbm_out, out_sems.at[0])
            push_state.start()
    else:
        state_out[...] = state[...]
        normed_from = state

    if do_conv:
        block = 32

        def norm_rows(i, carry):
            row = pl.multiple_of(i * block, block)
            x = normed_from[pl.ds(row, block), :].astype(jnp.float32)
            mean = jnp.mean(x, axis=1, keepdims=True)
            x = x - mean
            var = jnp.mean(x * x, axis=1, keepdims=True)
            y = x * (lax.rsqrt(var + EPSILON) * row_valid(row, block, 1))
            y = y.astype(jnp.bfloat16).astype(jnp.float32)
            for g in range(lane_groups):
                norm_s[g, pl.ds(row, block), :] = y[:, g * LANES : (g + 1) * LANES]
            return carry

        lax.fori_loop(0, act_rows // block, norm_rows, 0)
        for copy in tap_copies:
            copy.wait()
        out_rows = act_rows - taps_n
        edge = (out_rows - own) // 2
        mask_s[...] = row_valid(edge + taps_n // 2, own, LANES)
        tiles = out_rows // SUBLANES
        splits, run = conv_split(out_rows)

        def conv_lanes(g, carry):
            lanes = pl.ds(pl.multiple_of(g * LANES, LANES), LANES)
            for b in range(splits):
                base = b * (tiles // splits) * SUBLANES
                tap = [
                    jnp.broadcast_to(taps[k : k + 1, lanes].astype(jnp.float32), (SUBLANES, LANES))
                    for k in range(taps_n)
                ]
                acc = [None] * run
                for m in range(run + taps_n - 1):
                    v = norm_s[g, pl.ds(base + m, SUBLANES, stride=run), :]
                    for j in range(run):
                        if 0 <= m - j < taps_n:
                            term = tap[m - j] * v
                            acc[j] = term if acc[j] is None else acc[j] + term
                for j in range(run):
                    mix_s[pl.ds(base + j, SUBLANES, stride=run), :] = acc[j]
            mixed_out[:, lanes] = mix_s[:out_rows, :].astype(jnp.bfloat16)
            if far_out:
                pltpu.make_async_copy(
                    mixed_out.at[:, lanes], mixed_hbm_out.at[:, lanes], out_sems.at[1]
                ).start()
            mine = mix_s[edge : edge + own, :]
            masked = mine * mask_s[...]
            one = jnp.sum(masked, axis=0, keepdims=True)
            two = jnp.sum(masked * mine, axis=0, keepdims=True)
            both = jnp.concatenate([one, two], axis=0)
            for c in range(sums_out.shape[0]):
                sums_out[c, :, lanes] = both
            return carry

        lax.fori_loop(0, lane_groups, conv_lanes, 0)
        for copy in gb_copies + ([next_copy] if next_at is not None else []):
            copy.wait()
        if far_out:
            push_state.wait()
            pltpu.make_async_copy(mixed_out, mixed_hbm_out, out_sems.at[1]).wait()


def conv_split(out_rows):
    tiles = out_rows // SUBLANES
    splits = 1 if tiles <= 24 else 2
    run = tiles // splits
    return splits, run + (run % SUBLANES == 0)


def run_module(scal, state, z, own, layer, rim, copies, prev, do_conv, far, coming=None):
    width = state.shape[1]
    chunks = 6
    taps_n = 2 * rim
    do_mm = prev is not None
    vmem = pl.BlockSpec(memory_space=pltpu.VMEM)
    hbm = pl.BlockSpec(memory_space=pltpu.HBM)
    args, specs = [scal], [pl.BlockSpec(memory_space=pltpu.SMEM)]
    scratch = []
    group_at, blocks, held = 0, (), False
    act_rows = state.shape[0]
    if do_mm:
        mixed, sums, others, gb, parts, group_at = prev
        act_rows = mixed.shape[0]
        args += [mixed, sums, others, gb, *parts]
        held = group_at is None
        specs += [hbm if far[0] else vmem] + [vmem] * 3 + [vmem if held else hbm] * len(parts)
        rows = parts[0].shape[-2]
        if len(parts) > 1:
            blocks = tuple(p.shape[0] for p in parts)
        scratch += [
            pltpu.VMEM((act_rows, width), jnp.bfloat16),
            pltpu.VMEM((2, width), jnp.float32),
        ]
        if not held:
            scratch += [
                pltpu.VMEM((width // rows, rows, width), jnp.bfloat16),
                pltpu.SemaphoreType.DMA((max(chunks, sum(blocks)),)),
            ]
    args += [state, *z]
    specs += [hbm if far[0] else vmem, hbm, hbm]
    if coming is not None:
        args.append(coming[0])
        specs.append(hbm)
    shapes = [jax.ShapeDtypeStruct((act_rows, width), jnp.bfloat16)]
    if do_conv:
        out_rows = act_rows - taps_n
        splits, run = conv_split(out_rows)
        more = SUBLANES * (run - out_rows // SUBLANES // splits)
        scratch += [
            pltpu.VMEM((width // LANES, act_rows + more, LANES), jnp.float32),
            pltpu.VMEM((own, LANES), jnp.float32),
            pltpu.VMEM((out_rows + more, LANES), jnp.float32),
            pltpu.VMEM((taps_n, width), jnp.bfloat16),
        ]
        shapes += [
            jax.ShapeDtypeStruct((out_rows, width), jnp.bfloat16),
            jax.ShapeDtypeStruct((copies, 2, width), jnp.float32),
            jax.ShapeDtypeStruct((2, EXTRA, width), jnp.bfloat16),
        ]
    if coming is not None:
        blocks_n, _, rows, _ = coming[0].shape
        shapes.append(jax.ShapeDtypeStruct((blocks_n, rows, width), jnp.bfloat16))
    out_specs = [vmem] * len(shapes)
    scratch.append(pltpu.SemaphoreType.DMA((5,)))
    if far[0]:
        scratch += [
            pltpu.VMEM(mixed.shape, mixed.dtype),
            pltpu.VMEM(state.shape, state.dtype),
            pltpu.SemaphoreType.DMA((2,)),
        ]
    if far[1]:
        out_specs[0] = out_specs[1] = hbm
        shapes = [pltpu.HBM(a.shape, a.dtype) for a in shapes[:2]] + shapes[2:]
        scratch += [
            pltpu.VMEM(shapes[1].shape, shapes[1].dtype),
            pltpu.VMEM(shapes[0].shape, shapes[0].dtype),
            pltpu.SemaphoreType.DMA((2,)),
        ]
    plan = (
        do_mm, do_conv, layer, act_rows, own, layer * rim, chunks, group_at, taps_n, blocks, far,
        (held, None if coming is None else coming[1]),
    )
    args = [
        pltpu.with_memory_space_constraint(a, pltpu.HBM) if spec is hbm else a
        for a, spec in zip(args, specs)
    ]
    return pl.pallas_call(
        functools.partial(module_kernel, plan),
        out_shape=shapes,
        in_specs=specs,
        out_specs=out_specs,
        scratch_shapes=scratch,
        compiler_params=pltpu.CompilerParams(vmem_limit_bytes=32 << 20),
        name="module_step",
    )(*args)


SIDE = 4
STEPS = (0, 1, 3, 2)


def line_shift(steps, turned):
    pairs = []
    for p in range(SIDE):
        for q in range(SIDE):
            for core in range(2):
                to = (p, (q + steps) % SIDE) if core != turned else ((p + steps) % SIDE, q)
                pairs.append(((p * SIDE + q) * 2 + core, (to[0] * SIDE + to[1]) * 2 + core))
    return pairs


def along(x, steps):
    return lax.ppermute(x, ("ctx", "dp"), line_shift(steps, 0))


def across(x, steps):
    return lax.ppermute(x, ("ctx", "dp"), line_shift(steps, 1))


def plane_places():
    places = []
    for x in range(SIDE):
        for y in range(SIDE):
            by_core = [
                [((x - p) % SIDE * SIDE + (y - q) % SIDE) * 2 for q in STEPS for p in STEPS],
                [((x - q) % SIDE * SIDE + (y - p) % SIDE) * 2 + 1 for q in STEPS for p in STEPS],
            ]
            places += [by_core[0] + by_core[1], by_core[1] + by_core[0]]
    return jnp.array(places, jnp.int32)


STAGES = ((1, 4), (4, 8))


def shards(frames_in, lengths, depth_kernel, batch_gain, batch_bias, out_weight):
    layer_total = lax.axis_size("segment")
    ctx_count = lax.axis_size("ctx")
    segment_index = lax.axis_index("segment")
    ctx_index = lax.axis_index("ctx")
    dp_index = lax.axis_index("dp")
    frames_dev = frames_in.shape[2]
    kernel_size = depth_kernel.shape[1]
    rim = kernel_size // 2
    both = [(0, 1), (1, 0)]
    forward = [(i, i + 1) for i in range(ctx_count - 1)]
    backward = [(b, a) for a, b in forward]

    half_rows = out_weight.shape[1] // 2
    mine = lax.dynamic_slice_in_dim(out_weight[0], dp_index * half_rows, half_rows, 0)
    scales = jnp.where(dp_index == 0, batch_gain, batch_bias)
    upper = lax.reduce_precision(scales, 8, 7)
    scales = jnp.concatenate([upper, scales - upper], axis=0).astype(jnp.bfloat16)
    mine_taps = lax.dynamic_slice_in_dim(depth_kernel[0], dp_index * rim, rim, 0)
    pad = jnp.zeros((EXTRA - scales.shape[0], scales.shape[1]), jnp.bfloat16)
    mine = jnp.concatenate([mine, mine_taps.astype(jnp.bfloat16), scales, pad], axis=0)

    def shift(x, steps):
        pairs = [(i, (i + steps) % layer_total) for i in range(layer_total)]
        return lax.ppermute(x, "segment", pairs)

    def place(x, steps, row=0):
        at = (segment_index + steps) % layer_total
        return lax.dynamic_update_slice(ring, x[None], (at, row, 0))

    ring = jnp.broadcast_to(mine[None], (layer_total, *mine.shape))
    up = down = mine
    for steps in range(1, layer_total // 2):
        up, down = shift(up, 1), shift(down, -1)
        if steps == 1:
            lengths, up, down = lax.optimization_barrier((lengths, up, down))
        ring = place(up, -steps)
        ring = place(down, steps)
    ring = place(shift(up[:half_rows], 1), layer_total // 2)
    ring = place(shift(down[half_rows:], -1), layer_total // 2, half_rows)

    mine_len = lax.dynamic_slice_in_dim(lengths[0], segment_index, 1, 0)
    count = mine_len + lax.ppermute(mine_len, "dp", both)
    halo = rim * layer_total
    first = (ctx_index * frames_dev - halo).astype(jnp.int32)
    scal = [mine_len, first[None], count, dp_index[None]]
    at = ctx_index * 2 + dp_index
    places = lax.dynamic_index_in_dim(plane_places(), at, 0, keepdims=False)
    scal = jnp.concatenate([*scal, places])

    own = lax.dynamic_index_in_dim(frames_in[0], segment_index, 0, keepdims=False)
    low = lax.ppermute(own[frames_dev - halo :], "ctx", forward)
    high = lax.ppermute(own[:halo], "ctx", backward)
    low, high, _ = lax.optimization_barrier((low, high, up))
    state = jnp.concatenate([low, own, high], axis=0)

    ring, state, scal = lax.optimization_barrier((ring, state, scal))

    weights = {}

    def gather_stage(lo, hi, blocks):
        parts = [lax.all_gather(blocks[lo:hi, :half_rows], ("ctx", "dp"), axis=0)]
        for layer in range(lo, hi):
            weights[layer] = (parts, layer - lo)

    gather_stage(*STAGES[0], ring)
    line = ring[:1, :half_rows]
    line = [line] + [along(line, steps) for steps in STEPS[1:]]
    z = (ring, lax.ppermute(ring[:, half_rows:], "dp", both))
    waits = [lo for lo, _ in STAGES]

    prev = None
    for layer in range(layer_total):
        far = (layer - 1 in waits, layer in waits)
        coming = None
        if layer > 1 and layer not in waits:
            parts, group_at = weights[layer]
            coming = (parts[0], group_at)
        state, mixed, sums, gb, *fetched = run_module(
            scal, state, z, frames_dev, layer, rim, ctx_count, prev, True, far, coming
        )
        if layer == 0:
            line, sums = lax.optimization_barrier((line, sums))
            line, sums = lax.optimization_barrier((jnp.stack(line), sums))
            parts = [line] + [across(line, steps) for steps in STEPS[1:]]
        sums = lax.all_to_all(sums, "ctx", 0, 0, tiled=True)
        if layer == 0:
            parts, late, sums = lax.optimization_barrier((parts, ring, sums))
            for lo, hi in STAGES[1:]:
                gather_stage(lo, hi, late)
            weights[0] = (parts + [lax.ppermute(p, "dp", both) for p in parts], 0)
        others = lax.ppermute(sums, "dp", both)
        prev = (mixed, sums, others, gb, *((fetched, None) if fetched else weights[layer]))
    far = (False, False)
    (state,) = run_module(
        scal, state, z, frames_dev, layer_total, rim, ctx_count, prev, False, far
    )
    return state[None, None]


def solution(mesh):
    placed = (
        P("dp", None, "ctx", None),
        P("dp", None),
        P("segment", None, None),
        P("segment", None),
        P("segment", None),
        P("segment", "ctx", None),
    )
    return jax.shard_map(
        shards,
        mesh=mesh,
        in_specs=placed,
        out_specs=P("dp", "segment", "ctx", None),
        check_vma=False,
    )
```
